1024 devices in a mesh: grp: 16 (over z), dev: 64 (over y, x, core).
Axes of the slice: x: 4, y: 8, z: 16, core: 2. Of those that a mesh axis runs over, the one named last changes fastest.
Arguments:
- fields: float32 [4096, 6, 16, 256], P(('grp', 'dev')), may hold values from 0 to 1
- swap_dev: int32 [1024], P(('grp', 'dev')), may hold values from 0 to 1, as said below
- swap_grp: int32 [1024], P(('grp', 'dev')), may hold values from 0 to 1, as said below
- neighbors: int32 [4096, 6], P(('grp', 'dev')), may hold values from -1 to 4095, as said below
- orient: int32 [4096], P(('grp', 'dev')), may hold values from 0 to 7
Outputs:
- advanced: float32 [4096, 6, 16, 256], P(('grp', 'dev'))
The draws below stay inside these ranges and needn't reach their ends.
Inputs may be any that keep to these rules, and one draw needn't show every extreme that they name: `swap_dev`: equal on devices 2i and 2i+1 of each group. `swap_grp`: equal on the devices of one dev index in groups 2j and 2j+1. `neighbors`: adjacency is mutual: b names n across a face exactly when n names b across the opposite face. Neighbours across -x and -y lie on the same device or the previous dev index of the same group, across +x and +y on the same device or the next dev index of the same group; across -z and +z on the same dev index of the previous and the next group.
All inputs are finite; a program needn't handle non-finite values.
Results may differ from the reference program's by a relative error of at most 0.0001.
Values sent between devices are 32-bit elements; how exact they have to be, the bound alone decides.
A program may use at most 32 MiB of HBM per device.

```python
import math
import jax
import jax.numpy as jnp
from jax import lax

BS = 16
NPHASE = 4
NCONC = 2
NFIELD = 6
NORI = 8
STEPS = 2
SLOTS = 4
BLOCKS = 4096
N_GRP = 16
N_DEV = 64


def draw_swap_dev(key, part):
    bits = jax.random.randint(jax.random.fold_in(key, 101), (N_GRP, N_DEV // 2), 0, 2)
    return jnp.repeat(bits, 2, axis=1).reshape(N_GRP * N_DEV).astype(jnp.int32)


def draw_swap_grp(key, part):
    bits = jax.random.randint(jax.random.fold_in(key, 202), (N_GRP // 2, N_DEV), 0, 2)
    return jnp.repeat(bits, 2, axis=0).reshape(N_GRP * N_DEV).astype(jnp.int32)


def draw_neighbors(key, part):
    group_rows = SLOTS * N_DEV
    order = jnp.arange(group_rows)
    base = (jnp.arange(N_GRP) * group_rows).reshape(N_GRP, 1)
    columns = []
    for number in range(2):
        step_size = jax.random.randint(jax.random.fold_in(key, 303 + number), (N_GRP, 1), 1, SLOTS + 1)
        lower = order.reshape(1, group_rows) - step_size
        upper = order.reshape(1, group_rows) + step_size
        columns.append(jnp.where(lower >= 0, base + lower, -1))
        columns.append(jnp.where(upper < group_rows, base + upper, -1))
    subkeys = jax.random.split(jax.random.fold_in(key, 404), N_GRP * N_DEV)
    forward = jax.vmap(lambda one: jax.random.permutation(one, SLOTS))(subkeys).reshape(N_GRP, N_DEV, SLOTS).astype(jnp.int32)
    backward = jnp.argsort(forward, axis=2).astype(jnp.int32)
    groups = jnp.arange(N_GRP).reshape(N_GRP, 1, 1)
    devices = jnp.arange(N_DEV).reshape(1, N_DEV, 1)
    upper_z = jnp.where(groups < N_GRP - 1, ((groups + 1) * N_DEV + devices) * SLOTS + forward, -1)
    shifted = jnp.concatenate([backward[:1], backward[:-1]], axis=0)
    lower_z = jnp.where(groups > 0, ((groups - 1) * N_DEV + devices) * SLOTS + shifted, -1)
    columns.append(lower_z.reshape(N_GRP, group_rows))
    columns.append(upper_z.reshape(N_GRP, group_rows))
    table = jnp.stack(columns, axis=-1)
    return table.reshape(N_GRP * group_rows, 6).astype(jnp.int32)


def with_ends(values, rng, least, high):
    extent = values.shape
    index_at = [jax.random.randint(jax.random.fold_in(rng, axis), (), 0, extent[axis]) for axis in range(len(extent))]
    values = values.at[tuple(index_at)].set(least)
    longest = extent.index(max(extent))
    index_at[longest] = (index_at[longest] + 1) % extent[longest]
    return values.at[tuple(index_at)].set(high)


def block_levels(own_key, extent, pieces, smallest, high):
    level, own = 1.0, jax.random.fold_in(own_key, 6)
    for position, parts in pieces:
        steps = jnp.exp(jax.random.uniform(jax.random.fold_in(own, position), (parts,), jnp.float32, smallest / len(pieces), high / len(pieces)))
        level = level * jnp.repeat(steps, extent[position] // parts).reshape([-1 if axis == position else 1 for axis in range(len(extent))])
    return level


def setup_inputs(seed: int = 0) -> dict:
    splits = jax.random.split(jax.random.key(seed), 6)
    fields = jnp.clip(1.0 * jax.random.uniform(splits[0], (BLOCKS, NFIELD, BS, BS * BS), jnp.float32) ** block_levels(splits[0], (BLOCKS, NFIELD, BS, BS * BS), ((0, 1024),), -0.2, 0.2), 0.0, 1.0)
    swap_dev = draw_swap_dev(jax.random.fold_in(splits[5], 71), 0)
    swap_grp = draw_swap_grp(jax.random.fold_in(splits[5], 71), 0)
    neighbors = draw_neighbors(jax.random.fold_in(splits[5], 71), 0)
    orient = with_ends(jax.random.randint(splits[4], (BLOCKS,), 0, NORI), jax.random.fold_in(splits[4], 1), 0, NORI - 1).astype(jnp.int32)
    return dict(fields=fields, swap_dev=swap_dev, swap_grp=swap_grp, neighbors=neighbors, orient=orient)


phase_rate = 0.05
closure = 0.1
coupling = (0.5, -0.5, 1.0, -1.0)
conc_rates = (0.08, 0.04)


def coefficients(orient):
    theta = math.pi * orient.astype(jnp.float32) / NORI
    return 1.0 + 0.5 * jnp.cos(2.0 * theta), 1.0 - 0.5 * jnp.cos(2.0 * theta), 1.0 + 0.5 * jnp.sin(2.0 * theta)


def advance(inputs):
    block, ghosts, orient = inputs
    sums = []
    for axis in range(3):
        dim = 2 + axis
        lower = jnp.expand_dims(ghosts[2 * axis], dim)
        upper = jnp.expand_dims(ghosts[2 * axis + 1], dim)
        padded = jnp.concatenate([lower, block, upper], axis=dim)
        size = padded.shape[dim]
        sums.append(lax.slice_in_dim(padded, 2, size, axis=dim) + lax.slice_in_dim(padded, 0, size - 2, axis=dim))
    kx, ky, kz = coefficients(orient)
    kx = kx.reshape(-1, 1, 1, 1, 1)
    ky = ky.reshape(-1, 1, 1, 1, 1)
    kz = kz.reshape(-1, 1, 1, 1, 1)
    aniso = kx * (sums[0] - 2.0 * block) + ky * (sums[1] - 2.0 * block) + kz * (sums[2] - 2.0 * block)
    iso = sums[0] + sums[1] + sums[2] - 6.0 * block
    phases = block[:, :NPHASE]
    conc = block[:, NPHASE:]
    total = jnp.sum(phases, axis=1, keepdims=True)
    drive = conc[:, 0:1] - conc[:, 1:2]
    beta = jnp.array(coupling, jnp.float32).reshape(1, NPHASE, 1, 1, 1)
    rates = jnp.array(conc_rates, jnp.float32).reshape(1, NCONC, 1, 1, 1)
    well = phases * (1.0 - phases) * (1.0 - 2.0 * phases)
    new_phases = phases + phase_rate * (aniso[:, :NPHASE] - well + beta * drive * phases * (1.0 - phases) - closure * (total - 1.0))
    new_conc = conc + rates * iso[:, NPHASE:]
    return jnp.concatenate([new_phases, new_conc], axis=1)


def reference(fields, swap_dev, swap_grp, neighbors, orient):
    nfield = NPHASE + NCONC
    grid = fields.reshape(N_GRP, N_DEV, SLOTS, nfield, BS, BS * BS)
    flag_dev = swap_dev.reshape(N_GRP, N_DEV, 1, 1, 1)
    flag_grp = swap_grp.reshape(N_GRP, N_DEV, 1, 1, 1)
    index_dev = jnp.arange(N_DEV)
    partner_dev = index_dev + 1 - 2 * (index_dev % 2)
    index_grp = jnp.arange(N_GRP)
    partner_grp = index_grp + 1 - 2 * (index_grp % 2)
    last = grid[:, :, SLOTS - 1]
    last = jnp.where(flag_dev == 1, last[:, partner_dev], last)
    grid = grid.at[:, :, SLOTS - 1].set(last)
    first = grid[:, :, 0]
    first = jnp.where(flag_grp == 1, first[partner_grp], first)
    grid = grid.at[:, :, 0].set(first)
    blocks = grid.reshape(BLOCKS, nfield, BS, BS, BS)
    group_rows = SLOTS * N_DEV
    for step in range(STEPS):
        faces = [blocks[:, :, 0], blocks[:, :, BS - 1], blocks[:, :, :, 0], blocks[:, :, :, BS - 1], blocks[:, :, :, :, 0], blocks[:, :, :, :, BS - 1]]
        ghosts = []
        for face in range(6):
            opposite = face + 1 - 2 * (face % 2)
            target = neighbors[:, face]
            taken = faces[opposite][jnp.maximum(target, 0)]
            ghosts.append(jnp.where(target.reshape(-1, 1, 1, 1) < 0, faces[face], taken))
        stacked = jnp.stack(ghosts, axis=0).reshape(6, N_GRP, group_rows, nfield, BS, BS)
        stacked = jnp.moveaxis(stacked, 1, 0)
        result = lax.map(advance, (blocks.reshape(N_GRP, group_rows, nfield, BS, BS, BS), stacked, orient.reshape(N_GRP, group_rows)))
        blocks = result.reshape(BLOCKS, nfield, BS, BS, BS)
    return blocks.reshape(BLOCKS, nfield, BS, BS * BS)
```

```python
import functools
import math

import jax
import jax.numpy as jnp
import numpy as np
from jax import lax
from jax.experimental import pallas as pl
from jax.experimental.pallas import tpu as pltpu
from jax.sharding import PartitionSpec as P

MESH = pl.DeviceIdType.MESH
NORI = 8
EDGE = 16
SLOTS = 4
NFIELD = 6
LANES = 128
HALVES = 2
TILES = 3

phase_rate = 0.05
closure = 0.1
conc_rates = (0.08, 0.04)


def roll(v, shift, axis):
    shift %= v.shape[axis]
    return v if shift == 0 else pltpu.roll(v, shift, axis)


def rows_of(ref, half, tile, x):
    start = half * (NFIELD * SLOTS * EDGE) + tile * (8 * EDGE) + x
    flat = ref.reshape(HALVES * NFIELD * SLOTS * EDGE, LANES)
    return flat, pl.ds(start, 8, stride=EDGE)


def read_rows(ref, half, tile, x):
    flat, rows = rows_of(ref, half, tile, x)
    return flat[rows, :]


def write_rows(ref, half, tile, x, v):
    flat, rows = rows_of(ref, half, tile, x)
    flat[rows, :] = v


def kernel(
    n_grp, n_dev, fields, swap_dev, swap_grp, neighbors, orient, out,
    raw, moved, state0, state1, result, faces0, faces1, ghosts0, ghosts1, chosen,
    load_sem, store_sem, move_send, move_recv, send_sem, recv_sem,
):
    grp, dev = lax.axis_index("grp"), lax.axis_index("dev")
    rank = grp * n_dev + dev
    above_dev, below_dev = lax.rem(dev + 1, n_dev), lax.rem(dev + n_dev - 1, n_dev)
    above_grp, below_grp = lax.rem(grp + 1, n_grp), lax.rem(grp + n_grp - 1, n_grp)
    pair_dev = dev + 1 - 2 * lax.rem(dev, 2)
    pair_grp = grp + 1 - 2 * lax.rem(grp, 2)

    loads = []
    for slot in range(SLOTS):
        for half in range(HALVES):
            loads.append(
                pltpu.make_async_copy(
                    fields.at[slot, :, :, pl.ds(half * LANES, LANES)],
                    raw.at[half, :, slot],
                    load_sem.at[slot * HALVES + half],
                )
            )
    for copy in loads:
        copy.start()

    barrier = pltpu.get_barrier_semaphore()
    for target in ({"dev": above_dev}, {"dev": below_dev}, {"grp": above_grp}, {"grp": below_grp}):
        pl.semaphore_signal(barrier, inc=1, device_id=target, device_id_type=MESH)
    pl.semaphore_wait(barrier, 4)

    moves = []
    for slot, target in ((0, {"grp": pair_grp}), (SLOTS - 1, {"dev": pair_dev})):
        for half in range(HALVES):
            index = len(moves)
            moves.append(
                pltpu.make_async_remote_copy(
                    src_ref=fields.at[slot, :, :, pl.ds(half * LANES, LANES)],
                    dst_ref=moved.at[half, :, slot],
                    send_sem=move_send.at[index],
                    recv_sem=move_recv.at[index],
                    device_id=target,
                    device_id_type=MESH,
                )
            )
    for copy in moves:
        copy.start()

    row = lax.broadcasted_iota(jnp.int32, (8, LANES), 0)
    lane = lax.broadcasted_iota(jnp.int32, (8, LANES), 1)
    slot_of = row & 3
    z = lane & 15
    column = lane >> 4
    lane3 = lax.broadcasted_iota(jnp.int32, (TILES, 8, LANES), 2)
    z3 = lane3 & 15
    column3 = lane3 >> 4

    def per_slot(scalars):
        last = jnp.full((8, LANES), scalars[SLOTS - 1])
        for slot in range(SLOTS - 1):
            last = jnp.where(slot_of == slot, scalars[slot], last)
        return last

    angle = per_slot([orient[slot] for slot in range(SLOTS)])
    cosine = jnp.zeros((8, LANES), jnp.float32)
    sine = jnp.zeros((8, LANES), jnp.float32)
    for number in range(NORI):
        theta = np.float32(math.pi) * np.float32(number) / np.float32(NORI)
        cosine = jnp.where(angle == number, jnp.float32(np.cos(np.float32(2.0) * theta)), cosine)
        sine = jnp.where(angle == number, jnp.float32(np.sin(np.float32(2.0) * theta)), sine)
    scale_x = phase_rate * (1.0 + 0.5 * cosine)
    scale_y = phase_rate * (1.0 - 0.5 * cosine)
    scale_z = phase_rate * (1.0 + 0.5 * sine)
    scale_c = jnp.where(row < 4, jnp.float32(conc_rates[0]), jnp.float32(conc_rates[1]))
    self_p = 1.0 - 2.0 * (scale_x + scale_y + scale_z)
    self_c = 1.0 - 6.0 * scale_c

    picks = []
    for face in range(6):
        target = per_slot([neighbors[slot, face] for slot in range(SLOTS)])
        source_row = (row & 4) | (target & 3)
        picks.append((target < 0, (target >> 2) == rank, source_row))

    swapped_here = ((slot_of == 0) & (swap_grp[0] == 1)) | (
        (slot_of == SLOTS - 1) & (swap_dev[0] == 1)
    )

    for copy in loads:
        copy.wait()
    for x in range(EDGE):
        for half in range(HALVES):
            for tile in range(TILES):
                state0[x, half, tile] = read_rows(raw, half, tile, x)
    for copy in moves:
        copy.wait_recv()

    def pack(x, half, v, packs):
        y_low, y_high, z_low, z_high = packs
        if half == 0:
            y_low[x // 8] = jnp.where(column3 == x % 8, roll(v, 16 * x, 2), y_low[x // 8])
        else:
            y_high[x // 8] = jnp.where(column3 == x % 8, roll(v, 16 * x + 16, 2), y_high[x // 8])
        z_low[half] = jnp.where(z3 == x, roll(v, x, 2), z_low[half])
        z_high[half] = jnp.where(z3 == x, roll(v, x - 15, 2), z_high[half])

    def new_packs():
        zero = jnp.zeros((TILES, 8, LANES), jnp.float32)
        return [[zero, zero] for _ in range(4)]

    def send_copies(state, faces, ghosts, first):
        plan = (
            (state.at[EDGE - 1], 0, {"dev": above_dev}),
            (state.at[0], 1, {"dev": below_dev}),
            (faces.at[1], 2, {"dev": above_dev}),
            (faces.at[0], 3, {"dev": below_dev}),
            (faces.at[3], 4, {"grp": above_grp}),
            (faces.at[2], 5, {"grp": below_grp}),
        )
        return [
            pltpu.make_async_remote_copy(
                src_ref=source,
                dst_ref=ghosts.at[into],
                send_sem=send_sem.at[first + into],
                recv_sem=recv_sem.at[first + into],
                device_id=target,
                device_id_type=MESH,
            )
            for source, into, target in plan
        ]

    def store_packs(packs, faces):
        for number, pair in enumerate(packs):
            for half in range(HALVES):
                faces[number, half] = pair[half]

    def choose(state, faces, ghosts, copies):
        own = (state.at[0], state.at[EDGE - 1], faces.at[0], faces.at[1], faces.at[2], faces.at[3])
        for face in range(6):
            copies[face].wait_recv()
            outer, local, source_row = picks[face]
            mine, opposite = own[face], own[face + 1 - 2 * (face % 2)]
            for half in range(HALVES):
                for tile in range(TILES):
                    near = jnp.take_along_axis(opposite[half, tile], source_row, axis=0)
                    far = jnp.take_along_axis(ghosts[face, half, tile], source_row, axis=0)
                    chosen[face, half, tile] = jnp.where(
                        outer, mine[half, tile], jnp.where(local, near, far)
                    )

    def advance(state, x, half):
        v = state[x, half]
        other = state[x, 1 - half]
        below = chosen[0, half] if x == 0 else state[x - 1, half]
        above = chosen[1, half] if x == EDGE - 1 else state[x + 1, half]
        sum_x = below + above
        if half == 0:
            up = jnp.where(lane3 < 16, other, v)
            down = jnp.where(lane3 >= 112, roll(chosen[2, x // 8], 112 - 16 * x, 2), v)
        else:
            up = jnp.where(lane3 < 16, roll(chosen[3, x // 8], -16 * x, 2), v)
            down = jnp.where(lane3 >= 112, other, v)
        sum_y = roll(up, -16, 2) + roll(down, 16, 2)
        sum_z = jnp.where(z3 == 15, roll(chosen[5, half], 15 - x, 2), roll(v, -1, 2)) + jnp.where(
            z3 == 0, roll(chosen[4, half], -x, 2), roll(v, 1, 2)
        )
        p, c = v[:2], v[2]
        linear = scale_x * sum_x[:2] + scale_y * sum_y[:2] + scale_z * sum_z[:2] + self_p * p
        new_c = scale_c * (sum_x[2] + sum_y[2] + sum_z[2]) + self_c * c
        both = p[0] + p[1]
        total = both + roll(both, 4, 0)
        drive = c - roll(c, 4, 0)
        shared = (phase_rate * closure) - (phase_rate * closure) * total
        well = p - p * p
        bend = 2.0 * phase_rate * p - phase_rate
        new_0 = linear[0] + shared + well[0] * (bend[0] + (0.5 * phase_rate) * drive)
        new_1 = linear[1] + shared + well[1] * (bend[1] + phase_rate * drive)
        return new_0, new_1, new_c

    packs = new_packs()
    for x in range(EDGE):
        for half in range(HALVES):
            tiles = []
            for tile in range(TILES):
                arrived = read_rows(moved, half, tile, x)
                tiles.append(jnp.where(swapped_here, arrived, state0[x, half, tile]))
            v = jnp.stack(tiles)
            state0[x, half] = v
            pack(x, half, v, packs)
    store_packs(packs, faces0)
    first = send_copies(state0, faces0, ghosts0, 0)
    for copy in first:
        copy.start()
    choose(state0, faces0, ghosts0, first)

    packs = new_packs()
    for x in range(EDGE):
        for half in range(HALVES):
            v = jnp.stack(advance(state0, x, half))
            state1[x, half] = v
            pack(x, half, v, packs)
    store_packs(packs, faces1)
    second = send_copies(state1, faces1, ghosts1, 6)
    for copy in second:
        copy.start()
    choose(state1, faces1, ghosts1, second)

    stores = []
    for half in range(HALVES):
        for x in range(EDGE):
            for tile, v in enumerate(advance(state1, x, half)):
                write_rows(result, half, tile, x, v)
        for slot in range(SLOTS):
            stores.append(
                pltpu.make_async_copy(
                    result.at[half, :, slot],
                    out.at[slot, :, :, pl.ds(half * LANES, LANES)],
                    store_sem.at[half * SLOTS + slot],
                )
            )
            stores[-1].start()
    for copy in stores:
        copy.wait()
    for copy in moves + first + second:
        copy.wait_send()


def solution(mesh):
    n_grp, n_dev = mesh.shape["grp"], mesh.shape["dev"]

    def body(fields, swap_dev, swap_grp, neighbors, orient):
        block = (HALVES, NFIELD, SLOTS, EDGE, LANES)
        cells = (EDGE, HALVES, TILES, 8, LANES)
        return pl.pallas_call(
            functools.partial(kernel, n_grp, n_dev),
            out_shape=jax.ShapeDtypeStruct(fields.shape, fields.dtype),
            in_specs=[pl.BlockSpec(memory_space=pltpu.HBM)]
            + [pl.BlockSpec(memory_space=pltpu.SMEM)] * 4,
            out_specs=pl.BlockSpec(memory_space=pl.ANY),
            scratch_shapes=[
                pltpu.VMEM(block, jnp.float32),
                pltpu.VMEM(block, jnp.float32),
                pltpu.VMEM(cells, jnp.float32),
                pltpu.VMEM(cells, jnp.float32),
                pltpu.VMEM(block, jnp.float32),
                pltpu.VMEM((4,) + cells[1:], jnp.float32),
                pltpu.VMEM((4,) + cells[1:], jnp.float32),
                pltpu.VMEM((6,) + cells[1:], jnp.float32),
                pltpu.VMEM((6,) + cells[1:], jnp.float32),
                pltpu.VMEM((6,) + cells[1:], jnp.float32),
                pltpu.SemaphoreType.DMA((8,)),
                pltpu.SemaphoreType.DMA((8,)),
                pltpu.SemaphoreType.DMA((4,)),
                pltpu.SemaphoreType.DMA((4,)),
                pltpu.SemaphoreType.DMA((12,)),
                pltpu.SemaphoreType.DMA((12,)),
            ],
            compiler_params=pltpu.CompilerParams(
                collective_id=0, has_side_effects=True, vmem_limit_bytes=16 * 2**20
            ),
            name="phase_field_steps",
        )(fields, swap_dev, swap_grp, neighbors, orient)

    in_specs = (
        P(("grp", "dev"), None, None, None),
        P(("grp", "dev")),
        P(("grp", "dev")),
        P(("grp", "dev"), None),
        P(("grp", "dev")),
    )
    out_specs = P(("grp", "dev"), None, None, None)
    return jax.shard_map(body, mesh=mesh, in_specs=in_specs, out_specs=out_specs, check_vma=False)
```

```python
import functools
import math

import jax
import jax.numpy as jnp
import numpy as np
from jax import lax
from jax.experimental import pallas as pl
from jax.experimental.pallas import tpu as pltpu
from jax.sharding import PartitionSpec as P

MESH = pl.DeviceIdType.MESH
NORI = 8
EDGE = 16
SLOTS = 4
NFIELD = 6
LANES = 128
HALVES = 2
TILES = 3

phase_rate = 0.05
closure = 0.1
conc_rates = (0.08, 0.04)


def in_hbm(a):
    return pltpu.with_memory_space_constraint(a, pltpu.HBM)


def roll(v, shift):
    shift %= LANES
    return v if shift == 0 else pltpu.roll(v, shift, v.ndim - 1)


def rows_of(ref, half, tile, x):
    start = half * (NFIELD * SLOTS * EDGE) + tile * (8 * EDGE) + x
    flat = ref.reshape(HALVES * NFIELD * SLOTS * EDGE, LANES)
    return flat, pl.ds(start, 8, stride=EDGE)


def read_rows(ref, half, tile, x):
    flat, rows = rows_of(ref, half, tile, x)
    return flat[rows, :]


def write_rows(ref, half, tile, x, v):
    flat, rows = rows_of(ref, half, tile, x)
    flat[rows, :] = v


def kernel(
    n_grp, n_dev, fields, swap_dev, swap_grp, neighbors_hbm, orient_hbm, out,
    neighbors, orient,
    raw, moved, state0, state1, partial, result, faces0, faces1, ghosts0, ghosts1, chosen, walls_y, walls_z,
    small_sem, load_sem, store_sem, move_send, move_recv, send_sem, recv_sem,
):
    grp, dev = lax.axis_index("grp"), lax.axis_index("dev")
    rank = grp * n_dev + dev
    pair_dev = dev + 1 - 2 * lax.rem(dev, 2)
    pair_grp = grp + 1 - 2 * lax.rem(grp, 2)
    has_below_dev, has_above_dev = dev > 0, dev < n_dev - 1
    has_below_grp, has_above_grp = grp > 0, grp < n_grp - 1
    sides = (
        (has_below_dev, {"dev": dev - 1}),
        (has_above_dev, {"dev": dev + 1}),
        (has_below_grp, {"grp": grp - 1}),
        (has_above_grp, {"grp": grp + 1}),
    )

    barrier = pltpu.get_barrier_semaphore()
    for there, target in sides:

        @pl.when(there)
        def _():
            pl.semaphore_signal(barrier, inc=1, device_id=target, device_id_type=MESH)

    smalls = [
        pltpu.make_async_copy(source, into, small_sem.at[number])
        for number, (source, into) in enumerate(
            (
                (neighbors_hbm, neighbors),
                (orient_hbm, orient),
            )
        )
    ]
    loads = []
    for half in range(HALVES):
        for slot in range(SLOTS):
            loads.append(
                pltpu.make_async_copy(
                    fields.at[slot, :, :, pl.ds(half * LANES, LANES)],
                    raw.at[half, :, slot],
                    load_sem.at[half * SLOTS + slot],
                )
            )
    for copy in smalls + loads:
        copy.start()
    peers = [jnp.where(there, 1, 0) for there, _ in sides]
    pl.semaphore_wait(barrier, peers[0] + peers[1] + peers[2] + peers[3])

    moves = []
    for slot, target in ((0, {"grp": pair_grp}), (SLOTS - 1, {"dev": pair_dev})):
        for half in range(HALVES):
            index = len(moves)
            moves.append(
                pltpu.make_async_remote_copy(
                    src_ref=fields.at[slot, :, :, pl.ds(half * LANES, LANES)],
                    dst_ref=moved.at[half, :, slot],
                    send_sem=move_send.at[index],
                    recv_sem=move_recv.at[index],
                    device_id=target,
                    device_id_type=MESH,
                )
            )
    for copy in moves:
        copy.start()

    row = lax.broadcasted_iota(jnp.int32, (8, LANES), 0)
    lane = lax.broadcasted_iota(jnp.int32, (8, LANES), 1)
    slot_of = row & 3
    z = lane & 15
    column = lane >> 4
    low_y, high_y = lane < EDGE, lane >= LANES - EDGE

    def per_slot(scalars):
        last = jnp.full((8, LANES), scalars[SLOTS - 1])
        for slot in range(SLOTS - 1):
            last = jnp.where(slot_of == slot, scalars[slot], last)
        return last

    for copy in smalls:
        copy.wait()
    angle = per_slot([orient[slot] for slot in range(SLOTS)])
    cosine = jnp.zeros((8, LANES), jnp.float32)
    sine = jnp.zeros((8, LANES), jnp.float32)
    for number in range(NORI):
        theta = np.float32(math.pi) * np.float32(number) / np.float32(NORI)
        cosine = jnp.where(angle == number, jnp.float32(np.cos(np.float32(2.0) * theta)), cosine)
        sine = jnp.where(angle == number, jnp.float32(np.sin(np.float32(2.0) * theta)), sine)
    scale_x = phase_rate * (1.0 + 0.5 * cosine)
    scale_y = phase_rate * (1.0 - 0.5 * cosine)
    scale_z = phase_rate * (1.0 + 0.5 * sine)
    scale_c = jnp.where(row < 4, jnp.float32(conc_rates[0]), jnp.float32(conc_rates[1]))
    self_p = 1.0 - 2.0 * (scale_x + scale_y + scale_z)
    self_c = 1.0 - 6.0 * scale_c
    zero = jnp.zeros((8, LANES), jnp.float32)
    scales_x = (scale_x, scale_x, scale_c)
    scales_y = tuple(
        tuple(jnp.where(wall, v, zero) for v in (scale_y, scale_y, scale_c)) for wall in (low_y, high_y)
    )
    scales_z = tuple(jnp.where((z == 0) | (z == EDGE - 1), v, zero) for v in (scale_z, scale_z, scale_c))

    picks = []
    for face in range(6):
        target = per_slot([neighbors[slot, face] for slot in range(SLOTS)])
        source_row = (row & 4) | (target & 3)
        picks.append((target < 0, (target >> 2) == rank, source_row))

    swapped_here = ((slot_of == 0) & (swap_grp[0] == 1)) | (
        (slot_of == SLOTS - 1) & (swap_dev[0] == 1)
    )

    def pack_y(state, faces):
        for side in range(2):
            for tile in range(TILES):
                low, high = zero, zero
                for k in range(8):
                    x = side * 8 + k
                    both = jnp.where(lane < 64, state[x, 0, tile], state[x, 1, tile])
                    turned = roll(both, 16 * k)
                    low = jnp.where(column == k, turned, low)
                    high = jnp.where(column == (k + 7) % 8, turned, high)
                faces[0, side, tile] = low
                faces[1, side, tile] = roll(high, 16)

    def pack_z(state, faces):
        for half in range(HALVES):
            for tile in range(TILES):
                low, high = zero, zero
                for x in range(EDGE):
                    turned = roll(state[x, half, tile], x)
                    low = jnp.where(z == x, turned, low)
                    high = jnp.where(z == (x + 15) % 16, turned, high)
                faces[2, half, tile] = low
                faces[3, half, tile] = roll(high, -15)

    def exchange(state, faces, ghosts, first):
        plan = (
            (state.at[EDGE - 1], 0, 1),
            (state.at[0], 1, 0),
            (faces.at[1], 2, 1),
            (faces.at[0], 3, 0),
            (faces.at[3], 4, 3),
            (faces.at[2], 5, 2),
        )
        return [
            (
                pltpu.make_async_remote_copy(
                    src_ref=source,
                    dst_ref=ghosts.at[into],
                    send_sem=send_sem.at[first + into],
                    recv_sem=recv_sem.at[first + into],
                    device_id=sides[side][1],
                    device_id_type=MESH,
                ),
                sides[side][0],
                sides[side ^ 1][0],
            )
            for source, into, side in plan
        ]

    def start(copies):
        for copy, there, _ in copies:

            @pl.when(there)
            def _():
                copy.start()

    def choose(state, faces, ghosts, copies):
        own = (state.at[0], state.at[EDGE - 1], faces.at[0], faces.at[1], faces.at[2], faces.at[3])
        for copy, _, comes in copies:

            @pl.when(comes)
            def _():
                copy.wait_recv()

        def pick(face, part, tile):
            outer, local, source_row = picks[face]
            near = jnp.take_along_axis(own[face ^ 1][part, tile], source_row, axis=0)
            far = jnp.take_along_axis(ghosts[face, part, tile], source_row, axis=0)
            return jnp.where(outer, own[face][part, tile], jnp.where(local, near, far))

        for part in range(2):
            for tile in range(TILES):
                chosen[0, part, tile] = pick(0, part, tile)
                chosen[1, part, tile] = pick(1, part, tile)
                below, above = roll(pick(2, part, tile), 16), pick(3, part, tile)
                walls_y[0, part, tile] = jnp.where(column % 2 == 0, above, below)
                walls_y[1, part, tile] = jnp.where(column % 2 == 1, above, below)
                below, above = roll(pick(4, part, tile), -15), pick(5, part, tile)
                walls_z[0, part, tile] = jnp.where(z % 2 == 0, above, below)
                walls_z[1, part, tile] = jnp.where(z % 2 == 1, above, below)

    def prepare(state, x):
        v = [[state[x, half, tile] for tile in range(TILES)] for half in range(HALVES)]
        linear = [[None] * TILES for _ in range(HALVES)]
        for tile in range(TILES):
            ups = [roll(v[half][tile], -16) for half in range(HALVES)]
            downs = [roll(v[half][tile], 16) for half in range(HALVES)]
            sums_y = (
                jnp.where(high_y, ups[1], ups[0]) + jnp.where(low_y, zero, downs[0]),
                jnp.where(high_y, zero, ups[1]) + jnp.where(low_y, downs[0], downs[1]),
            )
            for half in range(HALVES):
                sum_z = jnp.where(z == EDGE - 1, zero, roll(v[half][tile], -1)) + jnp.where(
                    z == 0, zero, roll(v[half][tile], 1)
                )
                inner = [state[n, half, tile] for n in (x - 1, x + 1) if 0 <= n < EDGE]
                sum_x = inner[0] + inner[1] if len(inner) == 2 else inner[0]
                if tile < 2:
                    linear[half][tile] = (
                        scale_x * sum_x + scale_y * sums_y[half] + scale_z * sum_z + self_p * v[half][tile]
                    )
                else:
                    linear[half][tile] = scale_c * (sum_x + sums_y[half] + sum_z) + self_c * v[half][tile]
        for half in range(HALVES):
            p, q, c = v[half]
            both = p + q
            total = both + pltpu.roll(both, 4, 0)
            drive = c - pltpu.roll(c, 4, 0)
            shared = (phase_rate * closure) - (phase_rate * closure) * total
            partial[x, half, 0] = (
                linear[half][0]
                + shared
                + (p - p * p) * (2.0 * phase_rate * p - phase_rate + (0.5 * phase_rate) * drive)
            )
            partial[x, half, 1] = (
                linear[half][1]
                + shared
                + (q - q * q) * (2.0 * phase_rate * q - phase_rate + phase_rate * drive)
            )
            partial[x, half, 2] = linear[half][2]

    def finish(x, half, tile):
        v = partial[x, half, tile]
        v = v + scales_z[tile] * roll(walls_z[x % 2, half, tile], 15 - x)
        v = v + scales_y[half][tile] * roll(walls_y[x % 2, x // 8, tile], 16 * (7 - x % 8))
        if x == 0:
            v = v + scales_x[tile] * chosen[0, half, tile]
        if x == EDGE - 1:
            v = v + scales_x[tile] * chosen[1, half, tile]
        return v

    for copy in loads:
        copy.wait()
    for x in range(EDGE):
        for half in range(HALVES):
            for tile in range(TILES):
                state0[x, half, tile] = read_rows(raw, half, tile, x)
    for copy in moves:
        copy.wait_recv()
    order = (0, EDGE - 1, *range(1, EDGE - 1))
    for x in order:
        for half in range(HALVES):
            for tile in range(TILES):
                state0[x, half, tile] = jnp.where(
                    swapped_here, read_rows(moved, half, tile, x), state0[x, half, tile]
                )

    first = exchange(state0, faces0, ghosts0, 0)
    start(first[:2])
    pack_z(state0, faces0)
    start(first[4:])
    pack_y(state0, faces0)
    start(first[2:4])
    for x in range(EDGE):
        prepare(state0, x)
    choose(state0, faces0, ghosts0, first)

    for x in order:
        for half in range(HALVES):
            for tile in range(TILES):
                state1[x, half, tile] = finish(x, half, tile)
    second = exchange(state1, faces1, ghosts1, 6)
    start(second[:2])
    pack_z(state1, faces1)
    start(second[4:])
    pack_y(state1, faces1)
    start(second[2:4])
    for x in range(EDGE):
        prepare(state1, x)
    choose(state1, faces1, ghosts1, second)

    stores = []
    for half in range(HALVES):
        for x in range(EDGE):
            for tile in range(TILES):
                write_rows(result, half, tile, x, finish(x, half, tile))
        for slot in range(SLOTS):
            stores.append(
                pltpu.make_async_copy(
                    result.at[half, :, slot],
                    out.at[slot, :, :, pl.ds(half * LANES, LANES)],
                    store_sem.at[half * SLOTS + slot],
                )
            )
            stores[-1].start()
    for copy in stores:
        copy.wait()
    for copy in moves:
        copy.wait_send()
    for copy, there, _ in first + second:

        @pl.when(there)
        def _():
            copy.wait_send()


def solution(mesh):
    n_grp, n_dev = mesh.shape["grp"], mesh.shape["dev"]

    def body(fields, swap_dev, swap_grp, neighbors, orient):
        block = (HALVES, NFIELD, SLOTS, EDGE, LANES)
        plane = (HALVES, TILES, 8, LANES)
        smalls = (neighbors, orient)
        shapes = [block, block] + [(EDGE,) + plane] * 3 + [block]
        shapes += [(4,) + plane, (4,) + plane, (6,) + plane, (6,) + plane] + [(2,) + plane] * 3
        return pl.pallas_call(
            functools.partial(kernel, n_grp, n_dev),
            out_shape=jax.ShapeDtypeStruct(fields.shape, fields.dtype),
            in_specs=[pl.BlockSpec(memory_space=space) for space in (pl.ANY, pltpu.SMEM, pltpu.SMEM, pl.ANY, pl.ANY)],
            out_specs=pl.BlockSpec(memory_space=pl.ANY),
            scratch_shapes=[pltpu.SMEM(a.shape, a.dtype) for a in smalls]
            + [pltpu.VMEM(shape, jnp.float32) for shape in shapes]
            + [pltpu.SemaphoreType.DMA((n,)) for n in (2, 8, 8, 4, 4, 12, 12)],
            compiler_params=pltpu.CompilerParams(
                collective_id=0, has_side_effects=True, vmem_limit_bytes=16 * 2**20
            ),
            name="phase_field_steps",
        )(
            in_hbm(fields), swap_dev, swap_grp, *[in_hbm(a) for a in smalls]
        )

    in_specs = (
        P(("grp", "dev"), None, None, None),
        P(("grp", "dev")),
        P(("grp", "dev")),
        P(("grp", "dev"), None),
        P(("grp", "dev")),
    )
    out_specs = P(("grp", "dev"), None, None, None)
    return jax.shard_map(body, mesh=mesh, in_specs=in_specs, out_specs=out_specs, check_vma=False)
```

```python
import functools
import math

import jax
import jax.numpy as jnp
import numpy as np
from jax import lax
from jax.experimental import pallas as pl
from jax.experimental.pallas import tpu as pltpu
from jax.sharding import PartitionSpec as P

MESH = pl.DeviceIdType.MESH
NORI = 8
EDGE = 16
SLOTS = 4
NFIELD = 6
LANES = 128
HALVES = 2
TILES = 3

phase_rate = 0.05
closure = 0.1
conc_rates = (0.08, 0.04)


def in_hbm(a):
    return pltpu.with_memory_space_constraint(a, pltpu.HBM)


def roll(v, shift):
    shift %= LANES
    return v if shift == 0 else pltpu.roll(v, shift, v.ndim - 1)


def rows_of(ref, half, tile, x):
    start = half * (NFIELD * SLOTS * EDGE) + tile * (8 * EDGE) + x
    flat = ref.reshape(HALVES * NFIELD * SLOTS * EDGE, LANES)
    return flat, pl.ds(start, 8, stride=EDGE)


def read_rows(ref, half, tile, x):
    flat, rows = rows_of(ref, half, tile, x)
    return flat[rows, :]


def read_moved(moved, passed, odd, half, tile, x):
    last = read_rows(moved, half, tile, x)
    blocks = passed.reshape(2 * HALVES * NFIELD * EDGE, LANES)
    start = (odd * HALVES + half) * (NFIELD * EDGE) + 2 * tile * EDGE + x
    row = lax.broadcasted_iota(jnp.int32, (8, LANES), 0)
    upper = jnp.broadcast_to(blocks[pl.ds(start, 1), :], (8, LANES))
    lower = jnp.broadcast_to(blocks[pl.ds(start + EDGE, 1), :], (8, LANES))
    return jnp.where(row == 0, upper, jnp.where(row == 4, lower, last))


def write_rows(ref, half, tile, x, v):
    flat = ref.reshape(HALVES * NFIELD * SLOTS * EDGE, LANES)
    for part in range(2):
        start = (2 * tile + part) * 32 + (x // 8) * 16 + half * 8 + x % 8
        flat[pl.ds(start, 4, stride=NFIELD * 32), :] = v[4 * part : 4 * part + 4]


FACE_AT = (0, 13, 6, 19, 26, 35)
FLAGS_AT = (12, 25, 32, 41)
Z_BLOCK_AT = (33, 42)
FIRST_AT, LAST_AT = 44, 56
SHORT_AT = (0, 4, 2, 6, 8, 10)
PACKED = 68
RELAYED = 30


def kernel(
    n_grp, n_dev, fields, swap_dev, swap_grp, neighbors_hbm, orient_hbm, out,
    neighbors, orient,
    raw, moved, state0, state1, partial, packed, faces1, own1, far1, ghosts1, chosen, walls_y, walls_z,
    short3, beside, relayed, passed, outer3, outer0, beyond,
    small_sem, load_sem, send_sem, recv_sem, pass_send, pass_recv, first_send, first_recv,
):
    grp, dev = lax.axis_index("grp"), lax.axis_index("dev")
    rank = grp * n_dev + dev
    odd, odd_grp = lax.rem(dev, 2), lax.rem(grp, 2)
    even = odd == 0
    even_grp = odd_grp == 0
    pair_dev, pair_grp = dev + 1 - 2 * odd, grp + 1 - 2 * odd_grp
    out_dev, out_grp = dev - 1 + 2 * odd, grp - 1 + 2 * odd_grp
    relay = dev + 1 - odd
    has_below_dev, has_above_dev = dev > 0, dev < n_dev - 1
    has_below_grp, has_above_grp = grp > 0, grp < n_grp - 1
    has_outer = jnp.where(even, has_below_dev, has_above_dev)
    to_last = jnp.where(even, dev + 2, dev - 2)
    from_last = jnp.where(even, dev - 2, dev + 2)
    to_first = jnp.where(even_grp, grp + 2, grp - 2)
    from_first = jnp.where(even_grp, grp - 2, grp + 2)
    has_to_last = (to_last >= 0) & (to_last < n_dev)
    has_from_last = (from_last >= 0) & (from_last < n_dev)
    has_to_first = (to_first >= 0) & (to_first < n_grp)
    has_from_first = (from_first >= 0) & (from_first < n_grp)
    sides = (
        (has_below_dev, {"dev": dev - 1}),
        (has_above_dev, {"dev": dev + 1}),
        (has_below_grp, {"grp": grp - 1}),
        (has_above_grp, {"grp": grp + 1}),
    )
    above_relay = {"grp": grp + 1, "dev": relay}
    below_relay = {"grp": grp - 1, "dev": relay}
    pair_relay = {"grp": pair_grp, "dev": relay}
    outer_pair = {"grp": pair_grp, "dev": out_dev}
    is_odd = odd == 1

    barrier = pltpu.get_barrier_semaphore()
    sources = (
        sides[0], sides[1],
        (is_odd & has_below_grp, {"grp": grp - 1, "dev": dev}),
        (is_odd & has_above_grp, {"grp": grp + 1, "dev": dev}),
        (is_odd & has_below_grp, {"grp": grp - 1, "dev": dev - 1}),
        (is_odd & has_above_grp, {"grp": grp + 1, "dev": dev - 1}),
        (has_from_last, {"dev": from_last}),
        (has_outer, outer_pair),
        (has_from_first, {"grp": from_first}),
    )
    for there, target in sources:

        @pl.when(there)
        def _():
            pl.semaphore_signal(barrier, inc=1, device_id=target, device_id_type=MESH)

    smalls = [
        pltpu.make_async_copy(neighbors_hbm, neighbors, small_sem.at[0]),
        pltpu.make_async_copy(orient_hbm, orient, small_sem.at[1]),
    ]
    loads = []
    for half in range(HALVES):
        for slot in range(SLOTS):
            loads.append(
                pltpu.make_async_copy(
                    fields.at[slot, :, :, pl.ds(half * LANES, LANES)],
                    raw.at[half, :, slot],
                    load_sem.at[half * SLOTS + slot],
                )
            )
    for copy in loads + smalls:
        copy.start()

    row = lax.broadcasted_iota(jnp.int32, (8, LANES), 0)
    lane = lax.broadcasted_iota(jnp.int32, (8, LANES), 1)
    slot_of = row & 3
    z = lane & 15
    column = lane >> 4
    low_y, high_y = lane < EDGE, lane >= LANES - EDGE

    def per_slot(scalars):
        last = jnp.full((8, LANES), scalars[SLOTS - 1])
        for slot in range(SLOTS - 1):
            last = jnp.where(slot_of == slot, scalars[slot], last)
        return last

    for copy in smalls:
        copy.wait()
    angle = per_slot([orient[slot] for slot in range(SLOTS)])
    cosine = jnp.zeros((8, LANES), jnp.float32)
    sine = jnp.zeros((8, LANES), jnp.float32)
    for number in range(NORI):
        theta = np.float32(math.pi) * np.float32(number) / np.float32(NORI)
        cosine = jnp.where(angle == number, jnp.float32(np.cos(np.float32(2.0) * theta)), cosine)
        sine = jnp.where(angle == number, jnp.float32(np.sin(np.float32(2.0) * theta)), sine)
    scale_x = phase_rate * (1.0 + 0.5 * cosine)
    scale_y = phase_rate * (1.0 - 0.5 * cosine)
    scale_z = phase_rate * (1.0 + 0.5 * sine)
    scale_c = jnp.where(row < 4, jnp.float32(conc_rates[0]), jnp.float32(conc_rates[1]))
    self_p = 1.0 - 2.0 * (scale_x + scale_y + scale_z)
    self_c = 1.0 - 6.0 * scale_c
    zero = jnp.zeros((8, LANES), jnp.float32)
    scales_x = (scale_x, scale_x, scale_c)
    scales_y = tuple(
        tuple(jnp.where(wall, v, zero) for v in (scale_y, scale_y, scale_c)) for wall in (low_y, high_y)
    )
    scales_z = tuple(jnp.where((z == 0) | (z == EDGE - 1), v, zero) for v in (scale_z, scale_z, scale_c))

    picks = []
    for face in range(6):
        target = per_slot([neighbors[slot, face] for slot in range(SLOTS)])
        source_row = (row & 4) | (target & 3)
        picks.append((target < 0, (target >> 2) == rank, source_row))

    swapped_here = ((slot_of == 0) & (swap_grp[0] == 1)) | (
        (slot_of == SLOTS - 1) & (swap_dev[0] == 1)
    )

    def pack_y(state, put):
        for side in range(2):
            for tile in range(TILES):
                low, high = zero, zero
                for k in range(8):
                    x = side * 8 + k
                    both = jnp.where(lane < 64, state[x, 0, tile], state[x, 1, tile])
                    turned = roll(both, 16 * k)
                    low = jnp.where(column == k, turned, low)
                    high = jnp.where(column == (k + 7) % 8, turned, high)
                put(2, side, tile, low)
                put(3, side, tile, roll(high, 16))

    def pack_z(state, put):
        for half in range(HALVES):
            for tile in range(TILES):
                low, high = zero, zero
                for x in range(EDGE):
                    turned = roll(state[x, half, tile], x)
                    low = jnp.where(z == x, turned, low)
                    high = jnp.where(z == (x + 15) % 16, turned, high)
                put(4, half, tile, low)
                put(5, half, tile, roll(high, -15))

    def exchange(state, faces, ghosts):
        plan = (
            (state.at[EDGE - 1], 0, 1),
            (state.at[0], 1, 0),
            (faces.at[1], 2, 1),
            (faces.at[0], 3, 0),
            (faces.at[3], 4, 3),
            (faces.at[2], 5, 2),
        )
        return [
            (
                pltpu.make_async_remote_copy(
                    src_ref=source,
                    dst_ref=ghosts.at[into],
                    send_sem=send_sem.at[into],
                    recv_sem=recv_sem.at[into],
                    device_id=sides[side][1],
                    device_id_type=MESH,
                ),
                sides[side][0],
                sides[side ^ 1][0],
            )
            for source, into, side in plan
        ]

    def start(copies):
        for copy, there, _ in copies:

            @pl.when(there)
            def _():
                copy.start()

    def choose(own, ghosts):
        def pick(face, part, tile):
            outer, local, source_row = picks[face]
            near = jnp.take_along_axis(own(face ^ 1, part, tile), source_row, axis=0)
            far = jnp.take_along_axis(ghosts[face, part, tile], source_row, axis=0)
            return jnp.where(outer, own(face, part, tile), jnp.where(local, near, far))

        for part in range(2):
            for tile in range(TILES):
                chosen[0, part, tile] = pick(0, part, tile)
                chosen[1, part, tile] = pick(1, part, tile)
                below, above = roll(pick(2, part, tile), 16), pick(3, part, tile)
                walls_y[0, part, tile] = jnp.where(column % 2 == 0, above, below)
                walls_y[1, part, tile] = jnp.where(column % 2 == 1, above, below)
                below, above = roll(pick(4, part, tile), -15), pick(5, part, tile)
                walls_z[0, part, tile] = jnp.where(z % 2 == 0, above, below)
                walls_z[1, part, tile] = jnp.where(z % 2 == 1, above, below)

    def prepare(state, x):
        v = [[state[x, half, tile] for tile in range(TILES)] for half in range(HALVES)]
        linear = [[None] * TILES for _ in range(HALVES)]
        for tile in range(TILES):
            ups = [roll(v[half][tile], -16) for half in range(HALVES)]
            downs = [roll(v[half][tile], 16) for half in range(HALVES)]
            sums_y = (
                jnp.where(high_y, ups[1], ups[0]) + jnp.where(low_y, zero, downs[0]),
                jnp.where(high_y, zero, ups[1]) + jnp.where(low_y, downs[0], downs[1]),
            )
            for half in range(HALVES):
                sum_z = jnp.where(z == EDGE - 1, zero, roll(v[half][tile], -1)) + jnp.where(
                    z == 0, zero, roll(v[half][tile], 1)
                )
                inner = [state[n, half, tile] for n in (x - 1, x + 1) if 0 <= n < EDGE]
                sum_x = inner[0] + inner[1] if len(inner) == 2 else inner[0]
                if tile < 2:
                    linear[half][tile] = (
                        scale_x * sum_x + scale_y * sums_y[half] + scale_z * sum_z + self_p * v[half][tile]
                    )
                else:
                    linear[half][tile] = scale_c * (sum_x + sums_y[half] + sum_z) + self_c * v[half][tile]
        for half in range(HALVES):
            p, q, c = v[half]
            both = p + q
            total = both + pltpu.roll(both, 4, 0)
            drive = c - pltpu.roll(c, 4, 0)
            shared = (phase_rate * closure) - (phase_rate * closure) * total
            partial[x, half, 0] = (
                linear[half][0]
                + shared
                + (p - p * p) * (2.0 * phase_rate * p - phase_rate + (0.5 * phase_rate) * drive)
            )
            partial[x, half, 1] = (
                linear[half][1]
                + shared
                + (q - q * q) * (2.0 * phase_rate * q - phase_rate + phase_rate * drive)
            )
            partial[x, half, 2] = linear[half][2]

    def finish(x, half, tile):
        v = partial[x, half, tile]
        v = v + scales_z[tile] * roll(walls_z[x % 2, half, tile], 15 - x)
        v = v + scales_y[half][tile] * roll(walls_y[x % 2, x // 8, tile], 16 * (7 - x % 8))
        if x == 0:
            v = v + scales_x[tile] * chosen[0, half, tile]
        if x == EDGE - 1:
            v = v + scales_x[tile] * chosen[1, half, tile]
        return v

    for copy in loads:
        copy.wait()
    for x in range(EDGE):
        for half in range(HALVES):
            for tile in range(TILES):
                state0[x, half, tile] = read_rows(raw, half, tile, x)

    def put_packed(face, part, tile, v):
        packed[FACE_AT[face] + part * TILES + tile] = v

    def layer(face, part, tile):
        return packed[FACE_AT[face] + part * TILES + tile]

    for part in range(2):
        for tile in range(TILES):
            put_packed(0, part, tile, state0[0, part, tile])
            put_packed(1, part, tile, state0[EDGE - 1, part, tile])
    pack_y(state0, put_packed)
    pack_z(state0, put_packed)
    flags = jnp.where(swapped_here, 1.0, zero)
    for at in FLAGS_AT:
        packed[at] = flags
    for face in range(6):
        for part in range(2):
            tiles = [layer(face, part, tile) for tile in range(TILES)]
            first, last = tiles[0], zero
            for tile in range(TILES):
                shift = (tile - (SLOTS - 1)) % 8
                first = jnp.where(slot_of == tile, pltpu.roll(tiles[tile], tile, 0) if tile else tiles[0], first)
                last = jnp.where(slot_of == tile, pltpu.roll(tiles[tile], shift, 0), last)
            packed[FIRST_AT + SHORT_AT[face] + part] = first
            packed[LAST_AT + SHORT_AT[face] + part] = last
            if face >= 4:
                packed[Z_BLOCK_AT[face - 4] + part] = last

    count = jnp.int32(0)
    for there in (
        has_below_dev, has_above_dev, has_below_grp, has_above_grp, has_to_last, has_outer, has_to_first
    ):
        count = count + jnp.where(there, 1, 0)
    pl.semaphore_wait(barrier, count)

    always = rank >= 0
    sends = []

    def send(source, into, number, slot, there, target):
        copy = pltpu.make_async_remote_copy(
            src_ref=source,
            dst_ref=into,
            send_sem=first_send.at[number],
            recv_sem=first_recv.at[slot],
            device_id=target,
            device_id_type=MESH,
        )

        @pl.when(there)
        def _():
            copy.start()

        sends.append((copy, there))

    def received(into, slot, there):
        @pl.when(there)
        def _():
            pltpu.make_async_remote_copy(
                src_ref=into,
                dst_ref=into,
                send_sem=first_send.at[0],
                recv_sem=first_recv.at[slot],
                device_id={"dev": pair_dev},
                device_id_type=MESH,
            ).wait_recv()

    send(packed.at[pl.ds(26, 9)], relayed.at[odd, pl.ds(12, 9)], 0, 8 + 5 * odd, has_below_grp, below_relay)
    send(packed.at[pl.ds(35, 9)], relayed.at[odd, pl.ds(21, 9)], 1, 9 + 5 * odd, has_above_grp, above_relay)
    send(packed.at[pl.ds(FIRST_AT, 12)], relayed.at[odd, pl.ds(0, 12)], 2, 10 + 5 * odd, always, pair_relay)
    send(packed.at[pl.ds(0, 13)], beside.at[0], 3, 0, has_below_dev, sides[0][1])
    send(packed.at[pl.ds(13, 13)], beside.at[1], 4, 1, has_above_dev, sides[1][1])
    send(packed.at[pl.ds(LAST_AT, 12)], short3, 5, 2, always, {"dev": pair_dev})
    for half in range(HALVES):
        lanes = pl.ds(half * LANES, LANES)
        send(
            fields.at[0, :, :, lanes], passed.at[odd, half], 6 + half, 11 + half + 5 * odd, always, pair_relay
        )
    send(
        packed.at[pl.ds(LAST_AT + jnp.where(even, 4, 0), 4)], outer3, 8, 5, has_to_last, {"dev": to_last}
    )
    send(packed.at[pl.ds(FIRST_AT + jnp.where(even, 0, 4), 4)], outer0, 9, 6, has_outer, outer_pair)
    send(
        packed.at[pl.ds(FIRST_AT + jnp.where(even_grp, 10, 8), 2)], beyond, 10, 7, has_to_first, {"grp": to_first}
    )
    for half in range(HALVES):
        lanes = pl.ds(half * LANES, LANES)
        send(fields.at[SLOTS - 1, :, :, lanes], moved.at[half, :, SLOTS - 1], 11 + half, 3 + half, always, {"dev": pair_dev})

    passes = [
        pltpu.make_async_remote_copy(
            src_ref=ref,
            dst_ref=ref,
            send_sem=pass_send.at[number],
            recv_sem=pass_recv.at[number],
            device_id={"dev": pair_dev},
            device_id_type=MESH,
        )
        for number, ref in enumerate((relayed, passed.at[0]))
    ]
    for parity in range(2):
        base = 8 + 5 * parity
        received(relayed.at[parity, pl.ds(12, 9)], base, is_odd & has_above_grp)
        received(relayed.at[parity, pl.ds(21, 9)], base + 1, is_odd & has_below_grp)
        received(relayed.at[parity, pl.ds(0, 12)], base + 2, is_odd)

    @pl.when(is_odd)
    def _():
        passes[0].start()

    for half in range(HALVES):
        received(passed.at[0, half], 11 + half, is_odd)

    @pl.when(is_odd)
    def _():
        passes[1].start()

    for half in range(HALVES):
        received(passed.at[1, half], 16 + half, is_odd)

    @pl.when(even)
    def _():
        for copy in passes:
            copy.wait_recv()

    for half in range(HALVES):
        received(moved.at[half, :, SLOTS - 1], 3 + half, always)
    received(beside.at[0], 0, has_above_dev)
    received(beside.at[1], 1, has_below_dev)
    received(short3, 2, always)
    received(outer3, 5, has_from_last)
    received(outer0, 6, has_outer)
    received(beyond, 7, has_from_first)

    order = (0, EDGE - 1, *range(1, EDGE - 1))
    for x in order:
        for half in range(HALVES):
            for tile in range(TILES):
                state0[x, half, tile] = jnp.where(
                    swapped_here, read_moved(moved, passed, odd, half, tile, x), state0[x, half, tile]
                )
    for x in range(EDGE):
        prepare(state0, x)

    def spread(first, last, tile):
        return jnp.where(
            slot_of == 0, pltpu.roll(first, (8 - tile) % 8, 0) if tile else first, pltpu.roll(last, 3 - tile, 0)
        )

    is_first = slot_of == 0
    for face in range(6):
        at = SHORT_AT[face]
        for part in range(2):
            for tile in range(TILES):
                swapped = spread(relayed[odd, at + part], short3[at + part], tile)
                own1[face, part, tile] = jnp.where(swapped_here, swapped, layer(face, part, tile))
    for face in range(4):
        side = face % 2
        there = face ^ 1
        short = SHORT_AT[there] % 4
        near = even if side == 1 else is_odd
        landed = beside.at[1 - side]
        begin = 6 * (face // 2)
        flagged = landed[12] > 0.5
        for part in range(2):
            first = jnp.where(near, relayed[1 - odd, SHORT_AT[there] + part], outer0[short + part])
            for tile in range(TILES):
                mine = layer(there, part, tile)
                apart = spread(first, outer3[short + part], tile)
                swapped = jnp.where(is_first, apart, jnp.where(near, mine, apart))
                far1[face, part, tile] = jnp.where(flagged, swapped, landed[begin + part * TILES + tile])
    for face in (4, 5):
        there = face ^ 1
        begin = 12 if face == 5 else 21
        near = even_grp if face == 5 else odd_grp == 1
        flagged = relayed[odd, begin + 6] > 0.5
        for part in range(2):
            for tile in range(TILES):
                apart = spread(beyond[part], relayed[1 - odd, begin + 7 + part], tile)
                swapped = jnp.where(is_first & near, layer(there, part, tile), apart)
                far1[face, part, tile] = jnp.where(
                    flagged, swapped, relayed[odd, begin + part * TILES + tile]
                )
    choose(lambda face, part, tile: own1[face, part, tile], far1)

    for x in order:
        for half in range(HALVES):
            for tile in range(TILES):
                state1[x, half, tile] = finish(x, half, tile)

    def put_faces(face, part, tile, v):
        faces1[face - 2, part, tile] = v

    second = exchange(state1, faces1, ghosts1)
    start(second[:2])
    pack_y(state1, put_faces)
    start(second[2:4])
    pack_z(state1, put_faces)
    start(second[4:])
    for x in range(EDGE):
        prepare(state1, x)
    for copy, _, comes in second:

        @pl.when(comes)
        def _():
            copy.wait_recv()

    def own2(face, part, tile):
        if face < 2:
            return state1[(EDGE - 1) * face, part, tile]
        return faces1[face - 2, part, tile]

    choose(own2, ghosts1)

    for half in range(HALVES):
        for x in range(EDGE):
            for tile in range(TILES):
                write_rows(out, half, tile, x, finish(x, half, tile))

    @pl.when(is_odd)
    def _():
        for copy in passes:
            copy.wait_send()

    for copy, there, *_ in sends + second:

        @pl.when(there)
        def _():
            copy.wait_send()


def solution(mesh):
    n_grp, n_dev = mesh.shape["grp"], mesh.shape["dev"]

    def body(fields, swap_dev, swap_grp, neighbors, orient):
        block = (HALVES, NFIELD, SLOTS, EDGE, LANES)
        plane = (HALVES, TILES, 8, LANES)
        smalls = (neighbors, orient)
        cells = [(EDGE,) + plane] * 3
        shapes = [block, block, *cells, (PACKED, 8, LANES), (4,) + plane, *[(6,) + plane] * 3, *[(2,) + plane] * 3]
        shapes += [(12, 8, LANES), (2, 13, 8, LANES), (2, RELAYED, 8, LANES), (2, HALVES, NFIELD, EDGE, LANES)]
        shapes += [(4, 8, LANES), (4, 8, LANES), (2, 8, LANES)]
        new = pl.pallas_call(
            functools.partial(kernel, n_grp, n_dev),
            out_shape=jax.ShapeDtypeStruct((SLOTS, NFIELD, 2, HALVES, 8, LANES), fields.dtype),
            in_specs=[pl.BlockSpec(memory_space=space) for space in (pl.ANY, pltpu.SMEM, pltpu.SMEM, pl.ANY, pl.ANY)],
            out_specs=pl.BlockSpec(memory_space=pltpu.VMEM),
            scratch_shapes=[pltpu.SMEM(a.shape, a.dtype) for a in smalls]
            + [pltpu.VMEM(shape, jnp.float32) for shape in shapes]
            + [pltpu.SemaphoreType.DMA((n,)) for n in (2, 8, 6, 6, 2, 2, 13, 18)],
            compiler_params=pltpu.CompilerParams(
                collective_id=0, has_side_effects=True, vmem_limit_bytes=16 * 2**20
            ),
            name="phase_field_steps",
        )(
            in_hbm(fields), swap_dev, swap_grp, *[in_hbm(a) for a in smalls]
        )
        return new.transpose(0, 1, 2, 4, 3, 5).reshape(fields.shape)

    in_specs = (
        P(("grp", "dev"), None, None, None),
        P(("grp", "dev")),
        P(("grp", "dev")),
        P(("grp", "dev"), None),
        P(("grp", "dev")),
    )
    out_specs = P(("grp", "dev"), None, None, None)
    return jax.shard_map(body, mesh=mesh, in_specs=in_specs, out_specs=out_specs, check_vma=False)
```

```python
import functools
import math

import jax
import jax.numpy as jnp
import numpy as np
from jax import lax
from jax.experimental import pallas as pl
from jax.experimental.pallas import tpu as pltpu
from jax.sharding import PartitionSpec as P

MESH = pl.DeviceIdType.MESH
NORI = 8
EDGE = 16
SLOTS = 4
NFIELD = 6
LANES = 128
HALVES = 2
TILES = 3

phase_rate = 0.05
closure = 0.1
conc_rates = (0.08, 0.04)


def in_hbm(a):
    return pltpu.with_memory_space_constraint(a, pltpu.HBM)


def roll(v, shift):
    shift %= LANES
    return v if shift == 0 else pltpu.roll(v, shift, v.ndim - 1)


def rows_of(ref, half, tile, x):
    start = half * (NFIELD * SLOTS * EDGE) + tile * (8 * EDGE) + x
    flat = ref.reshape(HALVES * NFIELD * SLOTS * EDGE, LANES)
    return flat, pl.ds(start, 8, stride=EDGE)


def read_rows(ref, half, tile, x):
    flat, rows = rows_of(ref, half, tile, x)
    return flat[rows, :]


def read_moved(moved, passed, odd, half, tile, x):
    last = read_rows(moved, half, tile, x)
    blocks = passed.reshape(2 * HALVES * NFIELD * EDGE, LANES)
    start = (odd * HALVES + half) * (NFIELD * EDGE) + 2 * tile * EDGE + x
    row = lax.broadcasted_iota(jnp.int32, (8, LANES), 0)
    upper = jnp.broadcast_to(blocks[pl.ds(start, 1), :], (8, LANES))
    lower = jnp.broadcast_to(blocks[pl.ds(start + EDGE, 1), :], (8, LANES))
    return jnp.where(row == 0, upper, jnp.where(row == 4, lower, last))


def write_rows(ref, half, tile, x, v):
    flat = ref.reshape(HALVES * NFIELD * SLOTS * EDGE, LANES)
    for part in range(2):
        start = (2 * tile + part) * 32 + (x // 8) * 16 + half * 8 + x % 8
        flat[pl.ds(start, 4, stride=NFIELD * 32), :] = v[4 * part : 4 * part + 4]


FACE_AT = (0, 13, 6, 19, 26, 35)
FLAGS_AT = (12, 25, 32, 41)
Z_BLOCK_AT = (33, 42)
FIRST_AT, LAST_AT = 44, 56
SHORT_AT = (0, 4, 2, 6, 8, 10)
PACKED = 68
RELAYED = 30


def kernel(
    n_grp, n_dev, fields, swap_dev, swap_grp, neighbors_hbm, orient_hbm, out,
    neighbors, orient,
    raw, moved, state0, state1, partial, packed, faces1, own1, far1, ghosts1, chosen, walls_y, walls_z,
    short3, beside, relayed, passed, outer3, outer0, beyond,
    small_sem, load_sem, send_sem, recv_sem, pass_send, pass_recv, first_send, first_recv, ready_sem,
):
    grp, dev = lax.axis_index("grp"), lax.axis_index("dev")
    rank = grp * n_dev + dev
    odd, odd_grp = lax.rem(dev, 2), lax.rem(grp, 2)
    even = odd == 0
    even_grp = odd_grp == 0
    pair_dev, pair_grp = dev + 1 - 2 * odd, grp + 1 - 2 * odd_grp
    out_dev, out_grp = dev - 1 + 2 * odd, grp - 1 + 2 * odd_grp
    relay = dev + 1 - odd
    has_below_dev, has_above_dev = dev > 0, dev < n_dev - 1
    has_below_grp, has_above_grp = grp > 0, grp < n_grp - 1
    has_outer = jnp.where(even, has_below_dev, has_above_dev)
    to_last = jnp.where(even, dev + 2, dev - 2)
    from_last = jnp.where(even, dev - 2, dev + 2)
    to_first = jnp.where(even_grp, grp + 2, grp - 2)
    from_first = jnp.where(even_grp, grp - 2, grp + 2)
    has_to_last = (to_last >= 0) & (to_last < n_dev)
    has_from_last = (from_last >= 0) & (from_last < n_dev)
    has_to_first = (to_first >= 0) & (to_first < n_grp)
    has_from_first = (from_first >= 0) & (from_first < n_grp)
    sides = (
        (has_below_dev, {"dev": dev - 1}),
        (has_above_dev, {"dev": dev + 1}),
        (has_below_grp, {"grp": grp - 1}),
        (has_above_grp, {"grp": grp + 1}),
    )
    above_relay = {"grp": grp + 1, "dev": relay}
    below_relay = {"grp": grp - 1, "dev": relay}
    pair_relay = {"grp": pair_grp, "dev": relay}
    outer_pair = {"grp": pair_grp, "dev": out_dev}
    is_odd = odd == 1

    barrier = pltpu.get_barrier_semaphore()
    sources = (
        sides[0], (is_odd & has_above_dev, {"dev": dev + 1}),
        (is_odd & has_below_grp, {"grp": grp - 1, "dev": dev}),
        (is_odd & has_above_grp, {"grp": grp + 1, "dev": dev}),
        (is_odd & has_below_grp, {"grp": grp - 1, "dev": dev - 1}),
        (is_odd & has_above_grp, {"grp": grp + 1, "dev": dev - 1}),
        (has_from_last, {"dev": from_last}),
        (has_outer, outer_pair),
        (has_from_first, {"grp": from_first}),
    )
    for there, target in sources:

        @pl.when(there)
        def _():
            pl.semaphore_signal(barrier, inc=1, device_id=target, device_id_type=MESH)

    smalls = [
        pltpu.make_async_copy(neighbors_hbm, neighbors, small_sem.at[0]),
        pltpu.make_async_copy(orient_hbm, orient, small_sem.at[1]),
    ]
    loads = []
    for half in range(HALVES):
        for slot in range(SLOTS):
            loads.append(
                pltpu.make_async_copy(
                    fields.at[slot, :, :, pl.ds(half * LANES, LANES)],
                    raw.at[half, :, slot],
                    load_sem.at[half * SLOTS + slot],
                )
            )
    for copy in loads + smalls:
        copy.start()

    row = lax.broadcasted_iota(jnp.int32, (8, LANES), 0)
    lane = lax.broadcasted_iota(jnp.int32, (8, LANES), 1)
    slot_of = row & 3
    z = lane & 15
    column = lane >> 4
    low_y, high_y = lane < EDGE, lane >= LANES - EDGE

    def per_slot(scalars):
        last = jnp.full((8, LANES), scalars[SLOTS - 1])
        for slot in range(SLOTS - 1):
            last = jnp.where(slot_of == slot, scalars[slot], last)
        return last

    for copy in smalls:
        copy.wait()
    angle = per_slot([orient[slot] for slot in range(SLOTS)])
    cosine = jnp.zeros((8, LANES), jnp.float32)
    sine = jnp.zeros((8, LANES), jnp.float32)
    for number in range(NORI):
        theta = np.float32(math.pi) * np.float32(number) / np.float32(NORI)
        cosine = jnp.where(angle == number, jnp.float32(np.cos(np.float32(2.0) * theta)), cosine)
        sine = jnp.where(angle == number, jnp.float32(np.sin(np.float32(2.0) * theta)), sine)
    scale_x = phase_rate * (1.0 + 0.5 * cosine)
    scale_y = phase_rate * (1.0 - 0.5 * cosine)
    scale_z = phase_rate * (1.0 + 0.5 * sine)
    scale_c = jnp.where(row < 4, jnp.float32(conc_rates[0]), jnp.float32(conc_rates[1]))
    self_p = 1.0 - 2.0 * (scale_x + scale_y + scale_z)
    self_c = 1.0 - 6.0 * scale_c
    zero = jnp.zeros((8, LANES), jnp.float32)
    scales_x = (scale_x, scale_x, scale_c)
    scales_y = tuple(
        tuple(jnp.where(wall, v, zero) for v in (scale_y, scale_y, scale_c)) for wall in (low_y, high_y)
    )
    scales_z = tuple(jnp.where((z == 0) | (z == EDGE - 1), v, zero) for v in (scale_z, scale_z, scale_c))

    picks = []
    for face in range(6):
        target = per_slot([neighbors[slot, face] for slot in range(SLOTS)])
        source_row = (row & 4) | (target & 3)
        picks.append((target < 0, (target >> 2) == rank, source_row))

    swapped_here = ((slot_of == 0) & (swap_grp[0] == 1)) | (
        (slot_of == SLOTS - 1) & (swap_dev[0] == 1)
    )

    def pack_y(state, put):
        for side in range(2):
            for tile in range(TILES):
                low, high = zero, zero
                for k in range(8):
                    x = side * 8 + k
                    both = jnp.where(lane < 64, state[x, 0, tile], state[x, 1, tile])
                    turned = roll(both, 16 * k)
                    low = jnp.where(column == k, turned, low)
                    high = jnp.where(column == (k + 7) % 8, turned, high)
                put(2, side, tile, low)
                put(3, side, tile, roll(high, 16))

    def pack_z(state, put):
        for half in range(HALVES):
            for tile in range(TILES):
                low, high = zero, zero
                for x in range(EDGE):
                    turned = roll(state[x, half, tile], x)
                    low = jnp.where(z == x, turned, low)
                    high = jnp.where(z == (x + 15) % 16, turned, high)
                put(4, half, tile, low)
                put(5, half, tile, roll(high, -15))

    def exchange(state, faces, ghosts):
        plan = (
            (state.at[EDGE - 1], 0, 1),
            (state.at[0], 1, 0),
            (faces.at[1], 2, 1),
            (faces.at[0], 3, 0),
            (faces.at[3], 4, 3),
            (faces.at[2], 5, 2),
        )
        return [
            (
                pltpu.make_async_remote_copy(
                    src_ref=source,
                    dst_ref=ghosts.at[into],
                    send_sem=send_sem.at[into],
                    recv_sem=recv_sem.at[into],
                    device_id=sides[side][1],
                    device_id_type=MESH,
                ),
                sides[side][0],
                sides[side ^ 1][0],
            )
            for source, into, side in plan
        ]

    def start(copies):
        for copy, there, _ in copies:

            @pl.when(there)
            def _():
                copy.start()

    def choose(own, ghosts):
        def pick(face, part, tile):
            outer, local, source_row = picks[face]
            near = jnp.take_along_axis(own(face ^ 1, part, tile), source_row, axis=0)
            far = jnp.take_along_axis(ghosts[face, part, tile], source_row, axis=0)
            return jnp.where(outer, own(face, part, tile), jnp.where(local, near, far))

        for part in range(2):
            for tile in range(TILES):
                chosen[0, part, tile] = pick(0, part, tile)
                chosen[1, part, tile] = pick(1, part, tile)
                below, above = roll(pick(2, part, tile), 16), pick(3, part, tile)
                walls_y[0, part, tile] = jnp.where(column % 2 == 0, above, below)
                walls_y[1, part, tile] = jnp.where(column % 2 == 1, above, below)
                below, above = roll(pick(4, part, tile), -15), pick(5, part, tile)
                walls_z[0, part, tile] = jnp.where(z % 2 == 0, above, below)
                walls_z[1, part, tile] = jnp.where(z % 2 == 1, above, below)

    def prepare(state, x):
        v = [[state[x, half, tile] for tile in range(TILES)] for half in range(HALVES)]
        linear = [[None] * TILES for _ in range(HALVES)]
        for tile in range(TILES):
            ups = [roll(v[half][tile], -16) for half in range(HALVES)]
            downs = [roll(v[half][tile], 16) for half in range(HALVES)]
            sums_y = (
                jnp.where(high_y, ups[1], ups[0]) + jnp.where(low_y, zero, downs[0]),
                jnp.where(high_y, zero, ups[1]) + jnp.where(low_y, downs[0], downs[1]),
            )
            for half in range(HALVES):
                sum_z = jnp.where(z == EDGE - 1, zero, roll(v[half][tile], -1)) + jnp.where(
                    z == 0, zero, roll(v[half][tile], 1)
                )
                inner = [state[n, half, tile] for n in (x - 1, x + 1) if 0 <= n < EDGE]
                sum_x = inner[0] + inner[1] if len(inner) == 2 else inner[0]
                if tile < 2:
                    linear[half][tile] = (
                        scale_x * sum_x + scale_y * sums_y[half] + scale_z * sum_z + self_p * v[half][tile]
                    )
                else:
                    linear[half][tile] = scale_c * (sum_x + sums_y[half] + sum_z) + self_c * v[half][tile]
        for half in range(HALVES):
            p, q, c = v[half]
            both = p + q
            total = both + pltpu.roll(both, 4, 0)
            drive = c - pltpu.roll(c, 4, 0)
            shared = (phase_rate * closure) - (phase_rate * closure) * total
            partial[x, half, 0] = (
                linear[half][0]
                + shared
                + (p - p * p) * (2.0 * phase_rate * p - phase_rate + (0.5 * phase_rate) * drive)
            )
            partial[x, half, 1] = (
                linear[half][1]
                + shared
                + (q - q * q) * (2.0 * phase_rate * q - phase_rate + phase_rate * drive)
            )
            partial[x, half, 2] = linear[half][2]

    def finish(x, half, tile):
        v = partial[x, half, tile]
        v = v + scales_z[tile] * roll(walls_z[x % 2, half, tile], 15 - x)
        v = v + scales_y[half][tile] * roll(walls_y[x % 2, x // 8, tile], 16 * (7 - x % 8))
        if x == 0:
            v = v + scales_x[tile] * chosen[0, half, tile]
        if x == EDGE - 1:
            v = v + scales_x[tile] * chosen[1, half, tile]
        return v

    for copy in loads:
        copy.wait()
    for x in range(EDGE):
        for half in range(HALVES):
            for tile in range(TILES):
                state0[x, half, tile] = read_rows(raw, half, tile, x)

    def put_packed(face, part, tile, v):
        packed[FACE_AT[face] + part * TILES + tile] = v

    def layer(face, part, tile):
        return packed[FACE_AT[face] + part * TILES + tile]

    for part in range(2):
        for tile in range(TILES):
            put_packed(0, part, tile, state0[0, part, tile])
            put_packed(1, part, tile, state0[EDGE - 1, part, tile])
    pack_y(state0, put_packed)
    pack_z(state0, put_packed)
    flags = jnp.where(swapped_here, 1.0, zero)
    for at in FLAGS_AT:
        packed[at] = flags
    for face in range(6):
        for part in range(2):
            tiles = [layer(face, part, tile) for tile in range(TILES)]
            first, last = tiles[0], zero
            for tile in range(TILES):
                shift = (tile - (SLOTS - 1)) % 8
                first = jnp.where(slot_of == tile, pltpu.roll(tiles[tile], tile, 0) if tile else tiles[0], first)
                last = jnp.where(slot_of == tile, pltpu.roll(tiles[tile], shift, 0), last)
            packed[FIRST_AT + SHORT_AT[face] + part] = first
            packed[LAST_AT + SHORT_AT[face] + part] = last
            if face >= 4:
                packed[Z_BLOCK_AT[face - 4] + part] = last

    count = jnp.int32(0)
    for there in (
        has_below_dev & even, has_above_dev, has_below_grp, has_above_grp, has_to_last, has_outer, has_to_first
    ):
        count = count + jnp.where(there, 1, 0)
    pl.semaphore_wait(barrier, count)

    always = rank >= 0

    @pl.when(even)
    def _():
        pl.semaphore_signal(ready_sem, inc=1, device_id={"dev": pair_dev}, device_id_type=MESH)

    sends = []

    def send(source, into, number, slot, there, target):
        copy = pltpu.make_async_remote_copy(
            src_ref=source,
            dst_ref=into,
            send_sem=first_send.at[number],
            recv_sem=first_recv.at[slot],
            device_id=target,
            device_id_type=MESH,
        )

        @pl.when(there)
        def _():
            copy.start()

        sends.append((copy, there))

    def received(into, slot, there):
        @pl.when(there)
        def _():
            pltpu.make_async_remote_copy(
                src_ref=into,
                dst_ref=into,
                send_sem=first_send.at[0],
                recv_sem=first_recv.at[slot],
                device_id={"dev": pair_dev},
                device_id_type=MESH,
            ).wait_recv()

    send(packed.at[pl.ds(26, 9)], relayed.at[odd, pl.ds(12, 9)], 0, 8 + 5 * odd, has_below_grp, below_relay)
    send(packed.at[pl.ds(35, 9)], relayed.at[odd, pl.ds(21, 9)], 1, 9 + 5 * odd, has_above_grp, above_relay)
    send(packed.at[pl.ds(FIRST_AT, 12)], relayed.at[odd, pl.ds(0, 12)], 2, 10 + 5 * odd, always, pair_relay)
    for half in range(HALVES):
        lanes = pl.ds(half * LANES, LANES)
        send(
            fields.at[0, :, :, lanes], passed.at[odd, half], 6 + half, 11 + half + 5 * odd, always, pair_relay
        )
    send(packed.at[pl.ds(13 * odd, 13)], beside.at[odd], 3, odd, has_outer, {"dev": out_dev})
    send(
        packed.at[pl.ds(LAST_AT + jnp.where(even, 4, 0), 4)], outer3, 8, 5, has_to_last, {"dev": to_last}
    )
    send(packed.at[pl.ds(FIRST_AT + jnp.where(even, 0, 4), 4)], outer0, 9, 6, has_outer, outer_pair)
    send(
        packed.at[pl.ds(FIRST_AT + jnp.where(even_grp, 10, 8), 2)], beyond, 10, 7, has_to_first, {"grp": to_first}
    )

    @pl.when(is_odd)
    def _():
        pl.semaphore_wait(ready_sem, 1)

    send(packed.at[pl.ds(13 * (1 - odd), 13)], beside.at[1 - odd], 4, 1 - odd, always, {"dev": pair_dev})
    send(packed.at[pl.ds(LAST_AT, 12)], short3, 5, 2, always, {"dev": pair_dev})
    for half in range(HALVES):
        lanes = pl.ds(half * LANES, LANES)
        send(fields.at[SLOTS - 1, :, :, lanes], moved.at[half, :, SLOTS - 1], 11 + half, 3 + half, always, {"dev": pair_dev})

    passes = [
        pltpu.make_async_remote_copy(
            src_ref=ref,
            dst_ref=ref,
            send_sem=pass_send.at[number],
            recv_sem=pass_recv.at[number],
            device_id={"dev": pair_dev},
            device_id_type=MESH,
        )
        for number, ref in enumerate(
            (
                relayed.at[:, pl.ds(12, 9)],
                relayed.at[:, pl.ds(21, 9)],
                relayed.at[:, pl.ds(0, 12)],
                passed.at[0],
            )
        )
    ]

    def pass_on(number, there):
        @pl.when(there)
        def _():
            passes[number].start()

    def relay_layers(number, there):
        for parity in range(2):
            received(relayed.at[parity, pl.ds(12 + 9 * number, 9)], 8 + number + 5 * parity, there)
        pass_on(number, there)

    def relay_first(there):
        for parity in range(2):
            received(relayed.at[parity, pl.ds(0, 12)], 10 + 5 * parity, there)
        pass_on(2, there)

    def relay_block(there):
        for half in range(HALVES):
            received(passed.at[0, half], 11 + half, there)
        pass_on(3, there)

    relay_layers(0, is_odd & has_above_grp)
    relay_first(is_odd & even_grp)
    relay_block(is_odd & even_grp)
    for half in range(HALVES):
        received(passed.at[1, half], 16 + half, is_odd)

    @pl.when(even)
    def _():
        passes[3].wait_recv()

    for half in range(HALVES):
        received(moved.at[half, :, SLOTS - 1], 3 + half, always)

    order = (0, EDGE - 1, *range(1, EDGE - 1))
    for x in order:
        for half in range(HALVES):
            for tile in range(TILES):
                state0[x, half, tile] = jnp.where(
                    swapped_here, read_moved(moved, passed, odd, half, tile, x), state0[x, half, tile]
                )
    for x in range(EDGE):
        prepare(state0, x)

    relay_layers(1, is_odd & has_below_grp)
    relay_first(is_odd & (odd_grp == 1))
    for number, there in ((0, even & has_above_grp), (1, even & has_below_grp), (2, even)):

        @pl.when(there)
        def _():
            passes[number].wait_recv()

    received(beside.at[0], 0, has_above_dev)
    received(beside.at[1], 1, has_below_dev)
    received(short3, 2, always)
    received(outer3, 5, has_from_last)
    received(outer0, 6, has_outer)
    received(beyond, 7, has_from_first)

    def spread(first, last, tile):
        return jnp.where(
            slot_of == 0, pltpu.roll(first, (8 - tile) % 8, 0) if tile else first, pltpu.roll(last, 3 - tile, 0)
        )

    is_first = slot_of == 0
    for face in range(6):
        at = SHORT_AT[face]
        for part in range(2):
            for tile in range(TILES):
                swapped = spread(relayed[odd, at + part], short3[at + part], tile)
                own1[face, part, tile] = jnp.where(swapped_here, swapped, layer(face, part, tile))
    for face in range(4):
        side = face % 2
        there = face ^ 1
        short = SHORT_AT[there] % 4
        near = even if side == 1 else is_odd
        landed = beside.at[1 - side]
        begin = 6 * (face // 2)
        flagged = landed[12] > 0.5
        for part in range(2):
            first = jnp.where(near, relayed[1 - odd, SHORT_AT[there] + part], outer0[short + part])
            for tile in range(TILES):
                mine = layer(there, part, tile)
                apart = spread(first, outer3[short + part], tile)
                swapped = jnp.where(is_first, apart, jnp.where(near, mine, apart))
                far1[face, part, tile] = jnp.where(flagged, swapped, landed[begin + part * TILES + tile])
    for face in (4, 5):
        there = face ^ 1
        begin = 12 if face == 5 else 21
        near = even_grp if face == 5 else odd_grp == 1
        flagged = relayed[odd, begin + 6] > 0.5
        for part in range(2):
            for tile in range(TILES):
                apart = spread(beyond[part], relayed[1 - odd, begin + 7 + part], tile)
                swapped = jnp.where(is_first & near, layer(there, part, tile), apart)
                far1[face, part, tile] = jnp.where(
                    flagged, swapped, relayed[odd, begin + part * TILES + tile]
                )
    choose(lambda face, part, tile: own1[face, part, tile], far1)

    for x in order:
        for half in range(HALVES):
            for tile in range(TILES):
                state1[x, half, tile] = finish(x, half, tile)

    def put_faces(face, part, tile, v):
        faces1[face - 2, part, tile] = v

    second = exchange(state1, faces1, ghosts1)
    start(second[:2])
    pack_z(state1, put_faces)
    start(second[4:])
    pack_y(state1, put_faces)
    start(second[2:4])
    relay_block(is_odd & (odd_grp == 1))
    for x in range(EDGE):
        prepare(state1, x)
    for copy, _, comes in second:

        @pl.when(comes)
        def _():
            copy.wait_recv()

    def own2(face, part, tile):
        if face < 2:
            return state1[(EDGE - 1) * face, part, tile]
        return faces1[face - 2, part, tile]

    choose(own2, ghosts1)

    for half in range(HALVES):
        for x in range(EDGE):
            for tile in range(TILES):
                write_rows(out, half, tile, x, finish(x, half, tile))

    for number, there in (
        (0, is_odd & has_above_grp), (1, is_odd & has_below_grp), (2, is_odd), (3, is_odd)
    ):

        @pl.when(there)
        def _():
            passes[number].wait_send()

    for copy, there, *_ in sends + second:

        @pl.when(there)
        def _():
            copy.wait_send()


def solution(mesh):
    n_grp, n_dev = mesh.shape["grp"], mesh.shape["dev"]

    def body(fields, swap_dev, swap_grp, neighbors, orient):
        block = (HALVES, NFIELD, SLOTS, EDGE, LANES)
        plane = (HALVES, TILES, 8, LANES)
        smalls = (neighbors, orient)
        cells = [(EDGE,) + plane] * 3
        shapes = [block, block, *cells, (PACKED, 8, LANES), (4,) + plane, *[(6,) + plane] * 3, *[(2,) + plane] * 3]
        shapes += [(12, 8, LANES), (2, 13, 8, LANES), (2, RELAYED, 8, LANES), (2, HALVES, NFIELD, EDGE, LANES)]
        shapes += [(4, 8, LANES), (4, 8, LANES), (2, 8, LANES)]
        new = pl.pallas_call(
            functools.partial(kernel, n_grp, n_dev),
            out_shape=jax.ShapeDtypeStruct((SLOTS, NFIELD, 2, HALVES, 8, LANES), fields.dtype),
            in_specs=[pl.BlockSpec(memory_space=space) for space in (pl.ANY, pltpu.SMEM, pltpu.SMEM, pl.ANY, pl.ANY)],
            out_specs=pl.BlockSpec(memory_space=pltpu.VMEM),
            scratch_shapes=[pltpu.SMEM(a.shape, a.dtype) for a in smalls]
            + [pltpu.VMEM(shape, jnp.float32) for shape in shapes]
            + [pltpu.SemaphoreType.DMA((n,)) for n in (2, 8, 6, 6, 4, 4, 13, 18)]
            + [pltpu.SemaphoreType.REGULAR],
            compiler_params=pltpu.CompilerParams(
                collective_id=0, has_side_effects=True, vmem_limit_bytes=16 * 2**20
            ),
            name="phase_field_steps",
        )(
            in_hbm(fields), swap_dev, swap_grp, *[in_hbm(a) for a in smalls]
        )
        return new.transpose(0, 1, 2, 4, 3, 5).reshape(fields.shape)

    in_specs = (
        P(("grp", "dev"), None, None, None),
        P(("grp", "dev")),
        P(("grp", "dev")),
        P(("grp", "dev"), None),
        P(("grp", "dev")),
    )
    out_specs = P(("grp", "dev"), None, None, None)
    return jax.shard_map(body, mesh=mesh, in_specs=in_specs, out_specs=out_specs, check_vma=False)
```

```python
import functools
import math

import jax
import jax.numpy as jnp
import numpy as np
from jax import lax
from jax.experimental import pallas as pl
from jax.experimental.pallas import tpu as pltpu
from jax.sharding import PartitionSpec as P

MESH = pl.DeviceIdType.MESH
NORI = 8
EDGE = 16
SLOTS = 4
NFIELD = 6
LANES = 128
HALVES = 2
TILES = 3

phase_rate = 0.05
closure = 0.1
conc_rates = (0.08, 0.04)


def in_hbm(a):
    return pltpu.with_memory_space_constraint(a, pltpu.HBM)


def roll(v, shift):
    shift %= LANES
    return v if shift == 0 else pltpu.roll(v, shift, v.ndim - 1)


def rows_of(ref, half, tile, x):
    start = half * (NFIELD * SLOTS * EDGE) + tile * (8 * EDGE) + x
    flat = ref.reshape(HALVES * NFIELD * SLOTS * EDGE, LANES)
    return flat, pl.ds(start, 8, stride=EDGE)


def read_rows(ref, half, tile, x):
    flat, rows = rows_of(ref, half, tile, x)
    return flat[rows, :]


def read_moved(moved, passed, odd, half, tile, x):
    last = read_rows(moved, half, tile, x)
    blocks = passed.reshape(2 * HALVES * NFIELD * EDGE, LANES)
    start = (odd * HALVES + half) * (NFIELD * EDGE) + 2 * tile * EDGE + x
    row = lax.broadcasted_iota(jnp.int32, (8, LANES), 0)
    upper = jnp.broadcast_to(blocks[pl.ds(start, 1), :], (8, LANES))
    lower = jnp.broadcast_to(blocks[pl.ds(start + EDGE, 1), :], (8, LANES))
    return jnp.where(row == 0, upper, jnp.where(row == 4, lower, last))


def write_rows(ref, half, tile, x, v):
    flat = ref.reshape(HALVES * NFIELD * SLOTS * EDGE, LANES)
    for part in range(2):
        start = (2 * tile + part) * 32 + (x // 8) * 16 + half * 8 + x % 8
        flat[pl.ds(start, 4, stride=NFIELD * 32), :] = v[4 * part : 4 * part + 4]


FACE_AT = (0, 13, 6, 19, 26, 35)
FLAGS_AT = (12, 25, 32, 41)
Z_BLOCK_AT = (33, 42)
FIRST_AT, LAST_AT = 44, 56
SHORT_AT = (0, 4, 2, 6, 8, 10)
PACKED = 68
RELAYED = 30


def kernel(
    n_grp, n_dev, fields, swap_dev, swap_grp, neighbors_hbm, orient_hbm, out,
    neighbors, orient,
    raw, moved, state0, state1, partial, packed, faces1, own1, far1, ghosts1, picked, chosen, walls_y, walls_z,
    short3, beside, relayed, passed, outer3, outer0, beyond,
    small_sem, load_sem, send_sem, recv_sem, pass_send, pass_recv, first_send, first_recv, ready_sem,
):
    grp, dev = lax.axis_index("grp"), lax.axis_index("dev")
    rank = grp * n_dev + dev
    odd, odd_grp = lax.rem(dev, 2), lax.rem(grp, 2)
    even = odd == 0
    even_grp = odd_grp == 0
    pair_dev, pair_grp = dev + 1 - 2 * odd, grp + 1 - 2 * odd_grp
    out_dev, out_grp = dev - 1 + 2 * odd, grp - 1 + 2 * odd_grp
    relay = dev + 1 - odd
    has_below_dev, has_above_dev = dev > 0, dev < n_dev - 1
    has_below_grp, has_above_grp = grp > 0, grp < n_grp - 1
    has_outer = jnp.where(even, has_below_dev, has_above_dev)
    to_last = jnp.where(even, dev + 2, dev - 2)
    from_last = jnp.where(even, dev - 2, dev + 2)
    to_first = jnp.where(even_grp, grp + 2, grp - 2)
    from_first = jnp.where(even_grp, grp - 2, grp + 2)
    has_to_last = (to_last >= 0) & (to_last < n_dev)
    has_from_last = (from_last >= 0) & (from_last < n_dev)
    has_to_first = (to_first >= 0) & (to_first < n_grp)
    has_from_first = (from_first >= 0) & (from_first < n_grp)
    sides = (
        (has_below_dev, {"dev": dev - 1}),
        (has_above_dev, {"dev": dev + 1}),
        (has_below_grp, {"grp": grp - 1}),
        (has_above_grp, {"grp": grp + 1}),
    )
    above_relay = {"grp": grp + 1, "dev": relay}
    below_relay = {"grp": grp - 1, "dev": relay}
    pair_relay = {"grp": pair_grp, "dev": relay}
    outer_pair = {"grp": pair_grp, "dev": out_dev}
    is_odd = odd == 1

    barrier = pltpu.get_barrier_semaphore()
    sources = (
        sides[0], (is_odd & has_above_dev, {"dev": dev + 1}),
        (is_odd & has_below_grp, {"grp": grp - 1, "dev": dev}),
        (is_odd & has_above_grp, {"grp": grp + 1, "dev": dev}),
        (is_odd & has_below_grp, {"grp": grp - 1, "dev": dev - 1}),
        (is_odd & has_above_grp, {"grp": grp + 1, "dev": dev - 1}),
        (has_from_last, {"dev": from_last}),
        (has_outer, outer_pair),
        (has_from_first, {"grp": from_first}),
    )
    for there, target in sources:

        @pl.when(there)
        def _():
            pl.semaphore_signal(barrier, inc=1, device_id=target, device_id_type=MESH)

    smalls = [
        pltpu.make_async_copy(neighbors_hbm, neighbors, small_sem.at[0]),
        pltpu.make_async_copy(orient_hbm, orient, small_sem.at[1]),
    ]
    loads = []
    for half in range(HALVES):
        for slot in range(SLOTS):
            loads.append(
                pltpu.make_async_copy(
                    fields.at[slot, :, :, pl.ds(half * LANES, LANES)],
                    raw.at[half, :, slot],
                    load_sem.at[half * SLOTS + slot],
                )
            )
    for copy in loads + smalls:
        copy.start()

    row = lax.broadcasted_iota(jnp.int32, (8, LANES), 0)
    lane = lax.broadcasted_iota(jnp.int32, (8, LANES), 1)
    slot_of = row & 3
    z = lane & 15
    column = lane >> 4
    low_y, high_y = lane < EDGE, lane >= LANES - EDGE

    def per_slot(scalars):
        last = jnp.full((8, LANES), scalars[SLOTS - 1])
        for slot in range(SLOTS - 1):
            last = jnp.where(slot_of == slot, scalars[slot], last)
        return last

    for copy in smalls:
        copy.wait()
    angle = per_slot([orient[slot] for slot in range(SLOTS)])
    cosine = jnp.zeros((8, LANES), jnp.float32)
    sine = jnp.zeros((8, LANES), jnp.float32)
    for number in range(NORI):
        theta = np.float32(math.pi) * np.float32(number) / np.float32(NORI)
        cosine = jnp.where(angle == number, jnp.float32(np.cos(np.float32(2.0) * theta)), cosine)
        sine = jnp.where(angle == number, jnp.float32(np.sin(np.float32(2.0) * theta)), sine)
    scale_x = phase_rate * (1.0 + 0.5 * cosine)
    scale_y = phase_rate * (1.0 - 0.5 * cosine)
    scale_z = phase_rate * (1.0 + 0.5 * sine)
    scale_c = jnp.where(row < 4, jnp.float32(conc_rates[0]), jnp.float32(conc_rates[1]))
    self_p = 1.0 - 2.0 * (scale_x + scale_y + scale_z)
    self_c = 1.0 - 6.0 * scale_c
    zero = jnp.zeros((8, LANES), jnp.float32)
    scales_x = (scale_x, scale_x, scale_c)
    scales_y = tuple(
        tuple(jnp.where(wall, v, zero) for v in (scale_y, scale_y, scale_c)) for wall in (low_y, high_y)
    )
    scales_z = tuple(jnp.where((z == 0) | (z == EDGE - 1), v, zero) for v in (scale_z, scale_z, scale_c))

    picks = []
    for face in range(6):
        target = per_slot([neighbors[slot, face] for slot in range(SLOTS)])
        source_row = (row & 4) | (target & 3)
        picks.append((target < 0, (target >> 2) == rank, source_row))

    swapped_here = ((slot_of == 0) & (swap_grp[0] == 1)) | (
        (slot_of == SLOTS - 1) & (swap_dev[0] == 1)
    )

    def pack_y(state, put):
        for side in range(2):
            for tile in range(TILES):
                low, high = zero, zero
                for k in range(8):
                    x = side * 8 + k
                    both = jnp.where(lane < 64, state[x, 0, tile], state[x, 1, tile])
                    turned = roll(both, 16 * k)
                    low = jnp.where(column == k, turned, low)
                    high = jnp.where(column == (k + 7) % 8, turned, high)
                put(2, side, tile, low)
                put(3, side, tile, roll(high, 16))

    def pack_z(state, put):
        for half in range(HALVES):
            for tile in range(TILES):
                low, high = zero, zero
                for x in range(EDGE):
                    turned = roll(state[x, half, tile], x)
                    low = jnp.where(z == x, turned, low)
                    high = jnp.where(z == (x + 15) % 16, turned, high)
                put(4, half, tile, low)
                put(5, half, tile, roll(high, -15))

    def exchange(state, faces, ghosts):
        plan = (
            (state.at[EDGE - 1], 0, 1),
            (state.at[0], 1, 0),
            (faces.at[1], 2, 1),
            (faces.at[0], 3, 0),
            (faces.at[3], 4, 3),
            (faces.at[2], 5, 2),
        )
        return [
            (
                pltpu.make_async_remote_copy(
                    src_ref=source,
                    dst_ref=ghosts.at[into],
                    send_sem=send_sem.at[into],
                    recv_sem=recv_sem.at[into],
                    device_id=sides[side][1],
                    device_id_type=MESH,
                ),
                sides[side][0],
                sides[side ^ 1][0],
            )
            for source, into, side in plan
        ]

    def start(copies):
        for copy, there, _ in copies:

            @pl.when(there)
            def _():
                copy.start()

    def choose(own, ghosts, along="xyz"):
        def pick(face, part, tile):
            outer, local, source_row = picks[face]
            near = jnp.take_along_axis(own(face ^ 1, part, tile), source_row, axis=0)
            far = jnp.take_along_axis(ghosts[face, part, tile], source_row, axis=0)
            return jnp.where(outer, own(face, part, tile), jnp.where(local, near, far))

        for part in range(2):
            for tile in range(TILES):
                if along != "z":
                    chosen[0, part, tile] = pick(0, part, tile)
                    chosen[1, part, tile] = pick(1, part, tile)
                    below, above = pick(2, part, tile), pick(3, part, tile)
                    picked[0, part, tile], picked[1, part, tile] = below, above
                    below = roll(below, 16)
                    walls_y[0, part, tile] = jnp.where(column % 2 == 0, above, below)
                    walls_y[1, part, tile] = jnp.where(column % 2 == 1, above, below)
                if along != "xy":
                    below, above = pick(4, part, tile), pick(5, part, tile)
                    picked[2, part, tile], picked[3, part, tile] = below, above
                    below = roll(below, -15)
                    walls_z[0, part, tile] = jnp.where(z % 2 == 0, above, below)
                    walls_z[1, part, tile] = jnp.where(z % 2 == 1, above, below)

    def prepare(state, x):
        v = [[state[x, half, tile] for tile in range(TILES)] for half in range(HALVES)]
        linear = [[None] * TILES for _ in range(HALVES)]
        for tile in range(TILES):
            ups = [roll(v[half][tile], -16) for half in range(HALVES)]
            downs = [roll(v[half][tile], 16) for half in range(HALVES)]
            sums_y = (
                jnp.where(high_y, ups[1], ups[0]) + jnp.where(low_y, zero, downs[0]),
                jnp.where(high_y, zero, ups[1]) + jnp.where(low_y, downs[0], downs[1]),
            )
            for half in range(HALVES):
                sum_z = jnp.where(z == EDGE - 1, zero, roll(v[half][tile], -1)) + jnp.where(
                    z == 0, zero, roll(v[half][tile], 1)
                )
                inner = [state[n, half, tile] for n in (x - 1, x + 1) if 0 <= n < EDGE]
                sum_x = inner[0] + inner[1] if len(inner) == 2 else inner[0]
                if tile < 2:
                    linear[half][tile] = (
                        scale_x * sum_x + scale_y * sums_y[half] + scale_z * sum_z + self_p * v[half][tile]
                    )
                else:
                    linear[half][tile] = scale_c * (sum_x + sums_y[half] + sum_z) + self_c * v[half][tile]
        for half in range(HALVES):
            p, q, c = v[half]
            both = p + q
            total = both + pltpu.roll(both, 4, 0)
            drive = c - pltpu.roll(c, 4, 0)
            shared = (phase_rate * closure) - (phase_rate * closure) * total
            partial[x, half, 0] = (
                linear[half][0]
                + shared
                + (p - p * p) * (2.0 * phase_rate * p - phase_rate + (0.5 * phase_rate) * drive)
            )
            partial[x, half, 1] = (
                linear[half][1]
                + shared
                + (q - q * q) * (2.0 * phase_rate * q - phase_rate + phase_rate * drive)
            )
            partial[x, half, 2] = linear[half][2]

    def finish_xy(v, x, half, tile):
        v = v + scales_y[half][tile] * roll(walls_y[x % 2, x // 8, tile], 16 * (7 - x % 8))
        if x == 0:
            v = v + scales_x[tile] * chosen[0, half, tile]
        if x == EDGE - 1:
            v = v + scales_x[tile] * chosen[1, half, tile]
        return v

    def finish_z(v, x, half, tile):
        return v + scales_z[tile] * roll(walls_z[x % 2, half, tile], 15 - x)

    for copy in loads:
        copy.wait()
    for x in range(EDGE):
        for half in range(HALVES):
            for tile in range(TILES):
                state0[x, half, tile] = read_rows(raw, half, tile, x)

    def put_packed(face, part, tile, v):
        packed[FACE_AT[face] + part * TILES + tile] = v

    def layer(face, part, tile):
        return packed[FACE_AT[face] + part * TILES + tile]

    def shorten(face):
        for part in range(2):
            tiles = [layer(face, part, tile) for tile in range(TILES)]
            first, last = tiles[0], zero
            for tile in range(TILES):
                shift = (tile - (SLOTS - 1)) % 8
                first = jnp.where(slot_of == tile, pltpu.roll(tiles[tile], tile, 0) if tile else tiles[0], first)
                last = jnp.where(slot_of == tile, pltpu.roll(tiles[tile], shift, 0), last)
            packed[FIRST_AT + SHORT_AT[face] + part] = first
            packed[LAST_AT + SHORT_AT[face] + part] = last
            if face >= 4:
                packed[Z_BLOCK_AT[face - 4] + part] = last

    flags = jnp.where(swapped_here, 1.0, zero)
    for at in FLAGS_AT:
        packed[at] = flags
    pack_z(state0, put_packed)
    shorten(4)
    shorten(5)

    count = jnp.int32(0)
    for there in (
        has_below_dev & even, has_above_dev, has_below_grp, has_above_grp, has_to_last, has_outer, has_to_first
    ):
        count = count + jnp.where(there, 1, 0)
    pl.semaphore_wait(barrier, count)

    always = rank >= 0

    @pl.when(even)
    def _():
        pl.semaphore_signal(ready_sem, inc=1, device_id={"dev": pair_dev}, device_id_type=MESH)

    sends = []

    def send(source, into, number, slot, there, target):
        copy = pltpu.make_async_remote_copy(
            src_ref=source,
            dst_ref=into,
            send_sem=first_send.at[number],
            recv_sem=first_recv.at[slot],
            device_id=target,
            device_id_type=MESH,
        )

        @pl.when(there)
        def _():
            copy.start()

        sends.append((copy, there))

    def received(into, slot, there):
        @pl.when(there)
        def _():
            pltpu.make_async_remote_copy(
                src_ref=into,
                dst_ref=into,
                send_sem=first_send.at[0],
                recv_sem=first_recv.at[slot],
                device_id={"dev": pair_dev},
                device_id_type=MESH,
            ).wait_recv()

    send(packed.at[pl.ds(26, 9)], relayed.at[odd, pl.ds(12, 9)], 0, 8 + 5 * odd, has_below_grp, below_relay)
    send(packed.at[pl.ds(35, 9)], relayed.at[odd, pl.ds(21, 9)], 1, 9 + 5 * odd, has_above_grp, above_relay)

    for part in range(2):
        for tile in range(TILES):
            put_packed(0, part, tile, state0[0, part, tile])
            put_packed(1, part, tile, state0[EDGE - 1, part, tile])
    pack_y(state0, put_packed)
    for face in range(4):
        shorten(face)
    send(packed.at[pl.ds(FIRST_AT, 12)], relayed.at[odd, pl.ds(0, 12)], 2, 10 + 5 * odd, always, pair_relay)
    send(packed.at[pl.ds(13 * odd, 13)], beside.at[odd], 3, odd, has_outer, {"dev": out_dev})
    send(
        packed.at[pl.ds(LAST_AT + jnp.where(even, 4, 0), 4)], outer3, 8, 5, has_to_last, {"dev": to_last}
    )
    send(packed.at[pl.ds(FIRST_AT + jnp.where(even, 0, 4), 4)], outer0, 9, 6, has_outer, outer_pair)
    send(
        packed.at[pl.ds(FIRST_AT + jnp.where(even_grp, 10, 8), 2)], beyond, 10, 7, has_to_first, {"grp": to_first}
    )

    for half in range(HALVES):
        lanes = pl.ds(half * LANES, LANES)
        send(
            fields.at[0, :, :, lanes], passed.at[odd, half], 6 + half, 11 + half + 5 * odd, always, pair_relay
        )

    @pl.when(is_odd)
    def _():
        pl.semaphore_wait(ready_sem, 1)

    send(packed.at[pl.ds(13 * (1 - odd), 13)], beside.at[1 - odd], 4, 1 - odd, always, {"dev": pair_dev})
    send(packed.at[pl.ds(LAST_AT, 12)], short3, 5, 2, always, {"dev": pair_dev})
    for half in range(HALVES):
        lanes = pl.ds(half * LANES, LANES)
        send(fields.at[SLOTS - 1, :, :, lanes], moved.at[half, :, SLOTS - 1], 11 + half, 3 + half, always, {"dev": pair_dev})

    passes = [
        pltpu.make_async_remote_copy(
            src_ref=ref,
            dst_ref=ref,
            send_sem=pass_send.at[number],
            recv_sem=pass_recv.at[number],
            device_id={"dev": pair_dev},
            device_id_type=MESH,
        )
        for number, ref in enumerate(
            (
                relayed.at[:, pl.ds(12, 9)],
                relayed.at[:, pl.ds(21, 9)],
                relayed.at[:, pl.ds(0, 12)],
                passed.at[0],
            )
        )
    ]

    def pass_on(number, there):
        @pl.when(there)
        def _():
            passes[number].start()

    def relay_layers(number, there):
        for parity in range(2):
            received(relayed.at[parity, pl.ds(12 + 9 * number, 9)], 8 + number + 5 * parity, there)
        pass_on(number, there)

    def relay_first(there):
        received(relayed.at[0, pl.ds(0, 12)], 10, there)
        pass_on(2, there)

    def relay_block(there):
        for half in range(HALVES):
            received(passed.at[0, half], 11 + half, there)
        pass_on(3, there)

    relay_layers(0, is_odd & has_above_grp)
    received(relayed.at[1, pl.ds(0, 12)], 15, is_odd)
    relay_first(is_odd & even_grp)
    relay_block(is_odd & even_grp)
    for half in range(HALVES):
        received(passed.at[1, half], 16 + half, is_odd)

    @pl.when(even)
    def _():
        passes[3].wait_recv()

    for half in range(HALVES):
        received(moved.at[half, :, SLOTS - 1], 3 + half, always)

    order = (0, EDGE - 1, *range(1, EDGE - 1))
    for x in order:
        for half in range(HALVES):
            for tile in range(TILES):
                state0[x, half, tile] = jnp.where(
                    swapped_here, read_moved(moved, passed, odd, half, tile, x), state0[x, half, tile]
                )
    for x in range(EDGE):
        prepare(state0, x)

    def spread(first, last, tile):
        return jnp.where(
            slot_of == 0, pltpu.roll(first, (8 - tile) % 8, 0) if tile else first, pltpu.roll(last, 3 - tile, 0)
        )

    def put_faces(face, part, tile, v):
        faces1[face - 2, part, tile] = v

    pack_z(partial, put_faces)
    pack_y(partial, put_faces)

    received(short3, 2, always)

    @pl.when(even)
    def _():
        passes[2].wait_recv()

    for face in range(6):
        at = SHORT_AT[face]
        for part in range(2):
            for tile in range(TILES):
                swapped = spread(relayed[odd, at + part], short3[at + part], tile)
                own1[face, part, tile] = jnp.where(swapped_here, swapped, layer(face, part, tile))

    relay_layers(1, is_odd & has_below_grp)
    relay_first(is_odd & (odd_grp == 1))
    for number, there in ((0, even & has_above_grp), (1, even & has_below_grp)):

        @pl.when(there)
        def _():
            passes[number].wait_recv()

    received(beside.at[0], 0, has_above_dev)
    received(beside.at[1], 1, has_below_dev)
    received(outer3, 5, has_from_last)
    received(outer0, 6, has_outer)
    received(beyond, 7, has_from_first)

    is_first = slot_of == 0
    for face in range(4):
        side = face % 2
        there = face ^ 1
        short = SHORT_AT[there] % 4
        near = even if side == 1 else is_odd
        landed = beside.at[1 - side]
        begin = 6 * (face // 2)
        flagged = landed[12] > 0.5
        for part in range(2):
            first = jnp.where(near, relayed[1 - odd, SHORT_AT[there] + part], outer0[short + part])
            for tile in range(TILES):
                mine = layer(there, part, tile)
                apart = spread(first, outer3[short + part], tile)
                swapped = jnp.where(is_first, apart, jnp.where(near, mine, apart))
                far1[face, part, tile] = jnp.where(flagged, swapped, landed[begin + part * TILES + tile])
    for face in (4, 5):
        there = face ^ 1
        begin = 12 if face == 5 else 21
        near = even_grp if face == 5 else odd_grp == 1
        flagged = relayed[odd, begin + 6] > 0.5
        for part in range(2):
            for tile in range(TILES):
                apart = spread(beyond[part], relayed[1 - odd, begin + 7 + part], tile)
                swapped = jnp.where(is_first & near, layer(there, part, tile), apart)
                far1[face, part, tile] = jnp.where(
                    flagged, swapped, relayed[odd, begin + part * TILES + tile]
                )
    choose(lambda face, part, tile: own1[face, part, tile], far1)

    all_x, all_y, all_z = (scale_x, scale_x, scale_c), (scale_y, scale_y, scale_c), (scale_z, scale_z, scale_c)

    def lanes_of(v, index):
        return jnp.take_along_axis(v, index, axis=1)

    def z_layers(half, tile):
        scale, wall = all_x[tile], all_y[tile]
        for side in range(2):
            at = 15 * side
            index = 16 * (lane & 7) + at
            edge = jnp.where(
                (lane & 8) == 0,
                lanes_of(picked[half, 0, tile], index),
                lanes_of(picked[half, 1, tile], index),
            )
            v = faces1[2 + side, half, tile] + all_z[tile] * picked[2 + side, half, tile]
            v = v + jnp.where(high_y if half else low_y, wall * edge, zero)
            v = v + jnp.where(z == 0, scale * roll(chosen[0, half, tile], -at), zero)
            v = v + jnp.where(z == EDGE - 1, scale * roll(chosen[1, half, tile], 15 - at), zero)
            faces1[2 + side, half, tile] = v

    def y_layers(part, tile):
        scale, wall = all_x[tile], all_z[tile]
        for side in range(2):
            index = 112 * side + 8 * part + column
            v = faces1[side, part, tile] + all_y[tile] * picked[side, part, tile]
            v = v + jnp.where(z == 0, wall * lanes_of(picked[2, side, tile], index), zero)
            v = v + jnp.where(z == EDGE - 1, wall * lanes_of(picked[3, side, tile], index), zero)
            plane = roll(chosen[part, side, tile], 112 * part - 112 * side)
            v = v + jnp.where(high_y if part else low_y, scale * plane, zero)
            faces1[side, part, tile] = v

    second = exchange(state1, faces1, ghosts1)
    def advance_at(x):
        for half in range(HALVES):
            for tile in range(TILES):
                v = finish_xy(partial[x, half, tile], x, half, tile)
                state1[x, half, tile] = finish_z(v, x, half, tile)

    for x in order[:2]:
        advance_at(x)
    for part in range(2):
        for tile in range(TILES):
            y_layers(part, tile)
    start(second[:4])
    for part in range(2):
        for tile in range(TILES):
            z_layers(part, tile)
    start(second[4:])
    for x in order[2:]:
        advance_at(x)
    relay_block(is_odd & (odd_grp == 1))
    for x in range(EDGE):
        prepare(state1, x)
    def wait(copies):
        for copy, _, comes in copies:

            @pl.when(comes)
            def _():
                copy.wait_recv()

    def own2(face, part, tile):
        if face < 2:
            return state1[(EDGE - 1) * face, part, tile]
        return faces1[face - 2, part, tile]

    wait(second)
    choose(own2, ghosts1)

    for half in range(HALVES):
        for x in range(EDGE):
            for tile in range(TILES):
                v = finish_xy(partial[x, half, tile], x, half, tile)
                write_rows(out, half, tile, x, finish_z(v, x, half, tile))

    for number, there in (
        (0, is_odd & has_above_grp), (1, is_odd & has_below_grp), (2, is_odd), (3, is_odd)
    ):

        @pl.when(there)
        def _():
            passes[number].wait_send()

    for copy, there, *_ in sends + second:

        @pl.when(there)
        def _():
            copy.wait_send()


def solution(mesh):
    n_grp, n_dev = mesh.shape["grp"], mesh.shape["dev"]

    def body(fields, swap_dev, swap_grp, neighbors, orient):
        block = (HALVES, NFIELD, SLOTS, EDGE, LANES)
        plane = (HALVES, TILES, 8, LANES)
        smalls = (neighbors, orient)
        cells = [(EDGE,) + plane] * 3
        shapes = [block, block, *cells, (PACKED, 8, LANES), (4,) + plane, *[(6,) + plane] * 3, (4,) + plane, *[(2,) + plane] * 3]
        shapes += [(12, 8, LANES), (2, 13, 8, LANES), (2, RELAYED, 8, LANES), (2, HALVES, NFIELD, EDGE, LANES)]
        shapes += [(4, 8, LANES), (4, 8, LANES), (2, 8, LANES)]
        new = pl.pallas_call(
            functools.partial(kernel, n_grp, n_dev),
            out_shape=jax.ShapeDtypeStruct((SLOTS, NFIELD, 2, HALVES, 8, LANES), fields.dtype),
            in_specs=[pl.BlockSpec(memory_space=space) for space in (pl.ANY, pltpu.SMEM, pltpu.SMEM, pl.ANY, pl.ANY)],
            out_specs=pl.BlockSpec(memory_space=pltpu.VMEM),
            scratch_shapes=[pltpu.SMEM(a.shape, a.dtype) for a in smalls]
            + [pltpu.VMEM(shape, jnp.float32) for shape in shapes]
            + [pltpu.SemaphoreType.DMA((n,)) for n in (2, 8, 6, 6, 4, 4, 13, 18)]
            + [pltpu.SemaphoreType.REGULAR],
            compiler_params=pltpu.CompilerParams(
                collective_id=0, has_side_effects=True, vmem_limit_bytes=16 * 2**20
            ),
            name="phase_field_steps",
        )(
            in_hbm(fields), swap_dev, swap_grp, *[in_hbm(a) for a in smalls]
        )
        return new.transpose(0, 1, 2, 4, 3, 5).reshape(fields.shape)

    in_specs = (
        P(("grp", "dev"), None, None, None),
        P(("grp", "dev")),
        P(("grp", "dev")),
        P(("grp", "dev"), None),
        P(("grp", "dev")),
    )
    out_specs = P(("grp", "dev"), None, None, None)
    return jax.shard_map(body, mesh=mesh, in_specs=in_specs, out_specs=out_specs, check_vma=False)
```

```python
import functools
import math

import jax
import jax.numpy as jnp
import numpy as np
from jax import lax
from jax.experimental import pallas as pl
from jax.experimental.pallas import tpu as pltpu
from jax.sharding import PartitionSpec as P

MESH = pl.DeviceIdType.MESH
NORI = 8
EDGE = 16
SLOTS = 4
NFIELD = 6
LANES = 128
HALVES = 2
TILES = 3

phase_rate = 0.05
closure = 0.1
conc_rates = (0.08, 0.04)


def in_hbm(a):
    return pltpu.with_memory_space_constraint(a, pltpu.HBM)


def roll(v, shift):
    shift %= LANES
    return v if shift == 0 else pltpu.roll(v, shift, v.ndim - 1)


def rows_of(ref, half, tile, x):
    start = half * (NFIELD * SLOTS * EDGE) + tile * (8 * EDGE) + x
    flat = ref.reshape(HALVES * NFIELD * SLOTS * EDGE, LANES)
    return flat, pl.ds(start, 8, stride=EDGE)


def read_rows(ref, half, tile, x):
    flat, rows = rows_of(ref, half, tile, x)
    return flat[rows, :]


def read_moved(moved, passed, odd, half, tile, x):
    last = read_rows(moved, half, tile, x)
    blocks = passed.reshape(2 * HALVES * NFIELD * EDGE, LANES)
    start = (odd * HALVES + half) * (NFIELD * EDGE) + 2 * tile * EDGE + x
    row = lax.broadcasted_iota(jnp.int32, (8, LANES), 0)
    upper = jnp.broadcast_to(blocks[pl.ds(start, 1), :], (8, LANES))
    lower = jnp.broadcast_to(blocks[pl.ds(start + EDGE, 1), :], (8, LANES))
    return jnp.where(row == 0, upper, jnp.where(row == 4, lower, last))


def write_rows(ref, half, tile, x, v):
    flat = ref.reshape(HALVES * NFIELD * SLOTS * EDGE, LANES)
    for part in range(2):
        start = (2 * tile + part) * 32 + (x // 8) * 16 + half * 8 + x % 8
        flat[pl.ds(start, 4, stride=NFIELD * 32), :] = v[4 * part : 4 * part + 4]


FACE_AT = (0, 13, 6, 19, 26, 35)
FLAGS_AT = (12, 25, 32, 41)
Z_BLOCK_AT = (33, 42)
FIRST_AT, LAST_AT = 44, 56
SHORT_AT = (0, 4, 2, 6, 8, 10)
PACKED = 68
RELAYED = 30


def kernel(
    n_grp, n_dev, fields, swap_dev, swap_grp, neighbors_hbm, orient_hbm, out,
    neighbors, orient,
    raw, moved, state0, state1, partial, packed, faces1, own1, far1, ghosts1, picked, chosen, walls_y, walls_z,
    short3, beside, relayed, passed, outer3, outer0, beyond,
    small_sem, load_sem, send_sem, recv_sem, pass_send, pass_recv, first_send, first_recv, ready_sem,
):
    grp, dev = lax.axis_index("grp"), lax.axis_index("dev")
    rank = grp * n_dev + dev
    odd, odd_grp = lax.rem(dev, 2), lax.rem(grp, 2)
    even = odd == 0
    even_grp = odd_grp == 0
    pair_dev, pair_grp = dev + 1 - 2 * odd, grp + 1 - 2 * odd_grp
    out_dev, out_grp = dev - 1 + 2 * odd, grp - 1 + 2 * odd_grp
    relay = dev + 1 - odd
    has_below_dev, has_above_dev = dev > 0, dev < n_dev - 1
    has_below_grp, has_above_grp = grp > 0, grp < n_grp - 1
    has_outer = jnp.where(even, has_below_dev, has_above_dev)
    to_last = jnp.where(even, dev + 2, dev - 2)
    from_last = jnp.where(even, dev - 2, dev + 2)
    to_first = jnp.where(even_grp, grp + 2, grp - 2)
    from_first = jnp.where(even_grp, grp - 2, grp + 2)
    has_to_last = (to_last >= 0) & (to_last < n_dev)
    has_from_last = (from_last >= 0) & (from_last < n_dev)
    has_to_first = (to_first >= 0) & (to_first < n_grp)
    has_from_first = (from_first >= 0) & (from_first < n_grp)
    sides = (
        (has_below_dev, {"dev": dev - 1}),
        (has_above_dev, {"dev": dev + 1}),
        (has_below_grp, {"grp": grp - 1}),
        (has_above_grp, {"grp": grp + 1}),
    )
    above_relay = {"grp": grp + 1, "dev": relay}
    below_relay = {"grp": grp - 1, "dev": relay}
    pair_relay = {"grp": pair_grp, "dev": relay}
    outer_pair = {"grp": pair_grp, "dev": out_dev}
    is_odd = odd == 1

    barrier = pltpu.get_barrier_semaphore()
    sources = (
        sides[0], (is_odd & has_above_dev, {"dev": dev + 1}),
        (is_odd & has_below_grp, {"grp": grp - 1, "dev": dev}),
        (is_odd & has_above_grp, {"grp": grp + 1, "dev": dev}),
        (is_odd & has_below_grp, {"grp": grp - 1, "dev": dev - 1}),
        (is_odd & has_above_grp, {"grp": grp + 1, "dev": dev - 1}),
        (has_from_last, {"dev": from_last}),
        (has_outer, outer_pair),
        (has_from_first, {"grp": from_first}),
    )
    for there, target in sources:

        @pl.when(there)
        def _():
            pl.semaphore_signal(barrier, inc=1, device_id=target, device_id_type=MESH)

    smalls = [
        pltpu.make_async_copy(neighbors_hbm, neighbors, small_sem.at[0]),
        pltpu.make_async_copy(orient_hbm, orient, small_sem.at[1]),
    ]
    loads = []
    for half in range(HALVES):
        for slot in range(SLOTS):
            loads.append(
                pltpu.make_async_copy(
                    fields.at[slot, :, :, pl.ds(half * LANES, LANES)],
                    raw.at[half, :, slot],
                    load_sem.at[half * SLOTS + slot],
                )
            )
    for copy in loads + smalls:
        copy.start()

    row = lax.broadcasted_iota(jnp.int32, (8, LANES), 0)
    lane = lax.broadcasted_iota(jnp.int32, (8, LANES), 1)
    slot_of = row & 3
    z = lane & 15
    column = lane >> 4
    low_y, high_y = lane < EDGE, lane >= LANES - EDGE

    def per_slot(scalars):
        last = jnp.full((8, LANES), scalars[SLOTS - 1])
        for slot in range(SLOTS - 1):
            last = jnp.where(slot_of == slot, scalars[slot], last)
        return last

    for copy in smalls:
        copy.wait()
    angle = per_slot([orient[slot] for slot in range(SLOTS)])
    cosine = jnp.zeros((8, LANES), jnp.float32)
    sine = jnp.zeros((8, LANES), jnp.float32)
    for number in range(NORI):
        theta = np.float32(math.pi) * np.float32(number) / np.float32(NORI)
        cosine = jnp.where(angle == number, jnp.float32(np.cos(np.float32(2.0) * theta)), cosine)
        sine = jnp.where(angle == number, jnp.float32(np.sin(np.float32(2.0) * theta)), sine)
    scale_x = phase_rate * (1.0 + 0.5 * cosine)
    scale_y = phase_rate * (1.0 - 0.5 * cosine)
    scale_z = phase_rate * (1.0 + 0.5 * sine)
    scale_c = jnp.where(row < 4, jnp.float32(conc_rates[0]), jnp.float32(conc_rates[1]))
    self_p = 1.0 - 2.0 * (scale_x + scale_y + scale_z)
    self_c = 1.0 - 6.0 * scale_c
    zero = jnp.zeros((8, LANES), jnp.float32)
    scales_x = (scale_x, scale_x, scale_c)
    scales_y = tuple(
        tuple(jnp.where(wall, v, zero) for v in (scale_y, scale_y, scale_c)) for wall in (low_y, high_y)
    )
    scales_z = tuple(jnp.where((z == 0) | (z == EDGE - 1), v, zero) for v in (scale_z, scale_z, scale_c))

    picks = []
    for face in range(6):
        target = per_slot([neighbors[slot, face] for slot in range(SLOTS)])
        source_row = (row & 4) | (target & 3)
        picks.append((target < 0, (target >> 2) == rank, source_row))

    swapped_here = ((slot_of == 0) & (swap_grp[0] == 1)) | (
        (slot_of == SLOTS - 1) & (swap_dev[0] == 1)
    )

    def pack_y(state, put):
        for side in range(2):
            for tile in range(TILES):
                low, high = zero, zero
                for k in range(8):
                    x = side * 8 + k
                    both = jnp.where(lane < 64, state[x, 0, tile], state[x, 1, tile])
                    turned = roll(both, 16 * k)
                    low = jnp.where(column == k, turned, low)
                    high = jnp.where(column == (k + 7) % 8, turned, high)
                put(2, side, tile, low)
                put(3, side, tile, roll(high, 16))

    def pack_z(state, put):
        for half in range(HALVES):
            for tile in range(TILES):
                low, high = zero, zero
                for x in range(EDGE):
                    turned = roll(state[x, half, tile], x)
                    low = jnp.where(z == x, turned, low)
                    high = jnp.where(z == (x + 15) % 16, turned, high)
                put(4, half, tile, low)
                put(5, half, tile, roll(high, -15))

    def exchange(state, faces, ghosts):
        plan = (
            (state.at[EDGE - 1], 0, 1),
            (state.at[0], 1, 0),
            (faces.at[1], 2, 1),
            (faces.at[0], 3, 0),
            (faces.at[3], 4, 3),
            (faces.at[2], 5, 2),
        )
        return [
            (
                pltpu.make_async_remote_copy(
                    src_ref=source,
                    dst_ref=ghosts.at[into],
                    send_sem=send_sem.at[into],
                    recv_sem=recv_sem.at[into],
                    device_id=sides[side][1],
                    device_id_type=MESH,
                ),
                sides[side][0],
                sides[side ^ 1][0],
            )
            for source, into, side in plan
        ]

    def start(copies):
        for copy, there, _ in copies:

            @pl.when(there)
            def _():
                copy.start()

    def choose(own, ghosts, along="xyz"):
        def pick(face, part, tile):
            outer, local, source_row = picks[face]
            near = jnp.take_along_axis(own(face ^ 1, part, tile), source_row, axis=0)
            far = jnp.take_along_axis(ghosts[face, part, tile], source_row, axis=0)
            return jnp.where(outer, own(face, part, tile), jnp.where(local, near, far))

        for part in range(2):
            for tile in range(TILES):
                if along != "z":
                    chosen[0, part, tile] = pick(0, part, tile)
                    chosen[1, part, tile] = pick(1, part, tile)
                    below, above = pick(2, part, tile), pick(3, part, tile)
                    picked[0, part, tile], picked[1, part, tile] = below, above
                    below = roll(below, 16)
                    walls_y[0, part, tile] = jnp.where(column % 2 == 0, above, below)
                    walls_y[1, part, tile] = jnp.where(column % 2 == 1, above, below)
                if along != "xy":
                    below, above = pick(4, part, tile), pick(5, part, tile)
                    picked[2, part, tile], picked[3, part, tile] = below, above
                    below = roll(below, -15)
                    walls_z[0, part, tile] = jnp.where(z % 2 == 0, above, below)
                    walls_z[1, part, tile] = jnp.where(z % 2 == 1, above, below)

    def prepare(state, x):
        v = [[state[x, half, tile] for tile in range(TILES)] for half in range(HALVES)]
        linear = [[None] * TILES for _ in range(HALVES)]
        for tile in range(TILES):
            ups = [roll(v[half][tile], -16) for half in range(HALVES)]
            downs = [roll(v[half][tile], 16) for half in range(HALVES)]
            sums_y = (
                jnp.where(high_y, ups[1], ups[0]) + jnp.where(low_y, zero, downs[0]),
                jnp.where(high_y, zero, ups[1]) + jnp.where(low_y, downs[0], downs[1]),
            )
            for half in range(HALVES):
                sum_z = jnp.where(z == EDGE - 1, zero, roll(v[half][tile], -1)) + jnp.where(
                    z == 0, zero, roll(v[half][tile], 1)
                )
                inner = [state[n, half, tile] for n in (x - 1, x + 1) if 0 <= n < EDGE]
                sum_x = inner[0] + inner[1] if len(inner) == 2 else inner[0]
                if tile < 2:
                    linear[half][tile] = (
                        scale_x * sum_x + scale_y * sums_y[half] + scale_z * sum_z + self_p * v[half][tile]
                    )
                else:
                    linear[half][tile] = scale_c * (sum_x + sums_y[half] + sum_z) + self_c * v[half][tile]
        for half in range(HALVES):
            p, q, c = v[half]
            both = p + q
            total = both + pltpu.roll(both, 4, 0)
            drive = c - pltpu.roll(c, 4, 0)
            shared = (phase_rate * closure) - (phase_rate * closure) * total
            partial[x, half, 0] = (
                linear[half][0]
                + shared
                + (p - p * p) * (2.0 * phase_rate * p - phase_rate + (0.5 * phase_rate) * drive)
            )
            partial[x, half, 1] = (
                linear[half][1]
                + shared
                + (q - q * q) * (2.0 * phase_rate * q - phase_rate + phase_rate * drive)
            )
            partial[x, half, 2] = linear[half][2]

    def finish_xy(v, x, half, tile):
        v = v + scales_y[half][tile] * roll(walls_y[x % 2, x // 8, tile], 16 * (7 - x % 8))
        if x == 0:
            v = v + scales_x[tile] * chosen[0, half, tile]
        if x == EDGE - 1:
            v = v + scales_x[tile] * chosen[1, half, tile]
        return v

    def finish_z(v, x, half, tile):
        return v + scales_z[tile] * roll(walls_z[x % 2, half, tile], 15 - x)

    for copy in loads:
        copy.wait()
    for x in range(EDGE):
        for half in range(HALVES):
            for tile in range(TILES):
                state0[x, half, tile] = read_rows(raw, half, tile, x)

    def put_packed(face, part, tile, v):
        packed[FACE_AT[face] + part * TILES + tile] = v

    def layer(face, part, tile):
        return packed[FACE_AT[face] + part * TILES + tile]

    def shorten(face):
        for part in range(2):
            tiles = [layer(face, part, tile) for tile in range(TILES)]
            first, last = tiles[0], zero
            for tile in range(TILES):
                shift = (tile - (SLOTS - 1)) % 8
                first = jnp.where(slot_of == tile, pltpu.roll(tiles[tile], tile, 0) if tile else tiles[0], first)
                last = jnp.where(slot_of == tile, pltpu.roll(tiles[tile], shift, 0), last)
            packed[FIRST_AT + SHORT_AT[face] + part] = first
            packed[LAST_AT + SHORT_AT[face] + part] = last
            if face >= 4:
                packed[Z_BLOCK_AT[face - 4] + part] = last

    flags = jnp.where(swapped_here, 1.0, zero)
    for at in FLAGS_AT:
        packed[at] = flags
    for part in range(2):
        for tile in range(TILES):
            put_packed(0, part, tile, state0[0, part, tile])
            put_packed(1, part, tile, state0[EDGE - 1, part, tile])
    pack_y(state0, put_packed)
    for face in range(4):
        shorten(face)
    pack_z(state0, put_packed)
    shorten(4)
    shorten(5)

    count = jnp.int32(0)
    for there in (
        has_below_dev & even, has_above_dev, has_below_grp, has_above_grp, has_to_last, has_outer, has_to_first
    ):
        count = count + jnp.where(there, 1, 0)
    pl.semaphore_wait(barrier, count)

    always = rank >= 0

    @pl.when(even)
    def _():
        pl.semaphore_signal(ready_sem, inc=1, device_id={"dev": pair_dev}, device_id_type=MESH)

    sends = []

    def send(source, into, number, slot, there, target):
        copy = pltpu.make_async_remote_copy(
            src_ref=source,
            dst_ref=into,
            send_sem=first_send.at[number],
            recv_sem=first_recv.at[slot],
            device_id=target,
            device_id_type=MESH,
        )

        @pl.when(there)
        def _():
            copy.start()

        sends.append((copy, there))

    def received(into, slot, there):
        @pl.when(there)
        def _():
            pltpu.make_async_remote_copy(
                src_ref=into,
                dst_ref=into,
                send_sem=first_send.at[0],
                recv_sem=first_recv.at[slot],
                device_id={"dev": pair_dev},
                device_id_type=MESH,
            ).wait_recv()


    send(
        packed.at[pl.ds(LAST_AT + jnp.where(even, 4, 0), 4)], outer3, 8, 5, has_to_last, {"dev": to_last}
    )
    send(packed.at[pl.ds(FIRST_AT + jnp.where(even, 0, 4), 4)], outer0, 9, 6, has_outer, outer_pair)
    send(packed.at[pl.ds(26, 9)], relayed.at[odd, pl.ds(12, 9)], 0, 8 + 5 * odd, has_below_grp, below_relay)
    send(packed.at[pl.ds(35, 9)], relayed.at[odd, pl.ds(21, 9)], 1, 9 + 5 * odd, has_above_grp, above_relay)
    send(packed.at[pl.ds(FIRST_AT, 12)], relayed.at[odd, pl.ds(0, 12)], 2, 10 + 5 * odd, always, pair_relay)
    send(packed.at[pl.ds(13 * odd, 13)], beside.at[odd], 3, odd, has_outer, {"dev": out_dev})
    send(
        packed.at[pl.ds(FIRST_AT + jnp.where(even_grp, 10, 8), 2)], beyond, 10, 7, has_to_first, {"grp": to_first}
    )

    for half in range(HALVES):
        lanes = pl.ds(half * LANES, LANES)
        send(
            fields.at[0, :, :, lanes], passed.at[odd, half], 6 + half, 11 + half + 5 * odd, always, pair_relay
        )

    @pl.when(is_odd)
    def _():
        pl.semaphore_wait(ready_sem, 1)

    send(packed.at[pl.ds(13 * (1 - odd), 13)], beside.at[1 - odd], 4, 1 - odd, always, {"dev": pair_dev})
    send(packed.at[pl.ds(LAST_AT, 12)], short3, 5, 2, always, {"dev": pair_dev})
    for half in range(HALVES):
        lanes = pl.ds(half * LANES, LANES)
        send(fields.at[SLOTS - 1, :, :, lanes], moved.at[half, :, SLOTS - 1], 11 + half, 3 + half, always, {"dev": pair_dev})

    passes = [
        pltpu.make_async_remote_copy(
            src_ref=ref,
            dst_ref=ref,
            send_sem=pass_send.at[number],
            recv_sem=pass_recv.at[number],
            device_id={"dev": pair_dev},
            device_id_type=MESH,
        )
        for number, ref in enumerate(
            (
                relayed.at[:, pl.ds(12, 9)],
                relayed.at[:, pl.ds(21, 9)],
                relayed.at[:, pl.ds(0, 12)],
                passed.at[0],
            )
        )
    ]

    def pass_on(number, there):
        @pl.when(there)
        def _():
            passes[number].start()

    def relay_layers(number, there):
        for parity in range(2):
            received(relayed.at[parity, pl.ds(12 + 9 * number, 9)], 8 + number + 5 * parity, there)
        pass_on(number, there)

    def relay_first(there):
        received(relayed.at[0, pl.ds(0, 12)], 10, there)
        pass_on(2, there)

    def relay_block(there):
        for half in range(HALVES):
            received(passed.at[0, half], 11 + half, there)
        pass_on(3, there)

    relay_layers(0, is_odd & has_above_grp)
    received(relayed.at[1, pl.ds(0, 12)], 15, is_odd)
    relay_first(is_odd & even_grp)
    relay_block(is_odd & even_grp)
    for half in range(HALVES):
        received(passed.at[1, half], 16 + half, is_odd)

    @pl.when(even)
    def _():
        passes[3].wait_recv()

    for half in range(HALVES):
        received(moved.at[half, :, SLOTS - 1], 3 + half, always)

    order = (0, EDGE - 1, *range(1, EDGE - 1))
    for x in order:
        for half in range(HALVES):
            for tile in range(TILES):
                state0[x, half, tile] = jnp.where(
                    swapped_here, read_moved(moved, passed, odd, half, tile, x), state0[x, half, tile]
                )
    for x in range(EDGE):
        prepare(state0, x)

    def spread(first, last, tile):
        return jnp.where(
            slot_of == 0, pltpu.roll(first, (8 - tile) % 8, 0) if tile else first, pltpu.roll(last, 3 - tile, 0)
        )

    def put_faces(face, part, tile, v):
        faces1[face - 2, part, tile] = v

    pack_z(partial, put_faces)
    pack_y(partial, put_faces)

    received(short3, 2, always)

    @pl.when(even)
    def _():
        passes[2].wait_recv()

    for face in range(6):
        at = SHORT_AT[face]
        for part in range(2):
            for tile in range(TILES):
                swapped = spread(relayed[odd, at + part], short3[at + part], tile)
                own1[face, part, tile] = jnp.where(swapped_here, swapped, layer(face, part, tile))

    relay_layers(1, is_odd & has_below_grp)
    relay_first(is_odd & (odd_grp == 1))
    for number, there in ((0, even & has_above_grp), (1, even & has_below_grp)):

        @pl.when(there)
        def _():
            passes[number].wait_recv()

    received(beside.at[0], 0, has_above_dev)
    received(beside.at[1], 1, has_below_dev)
    received(outer3, 5, has_from_last)
    received(outer0, 6, has_outer)
    received(beyond, 7, has_from_first)

    is_first = slot_of == 0
    for face in range(4):
        side = face % 2
        there = face ^ 1
        short = SHORT_AT[there] % 4
        near = even if side == 1 else is_odd
        landed = beside.at[1 - side]
        begin = 6 * (face // 2)
        flagged = landed[12] > 0.5
        for part in range(2):
            first = jnp.where(near, relayed[1 - odd, SHORT_AT[there] + part], outer0[short + part])
            for tile in range(TILES):
                mine = layer(there, part, tile)
                apart = spread(first, outer3[short + part], tile)
                swapped = jnp.where(is_first, apart, jnp.where(near, mine, apart))
                far1[face, part, tile] = jnp.where(flagged, swapped, landed[begin + part * TILES + tile])
    for face in (4, 5):
        there = face ^ 1
        begin = 12 if face == 5 else 21
        near = even_grp if face == 5 else odd_grp == 1
        flagged = relayed[odd, begin + 6] > 0.5
        for part in range(2):
            for tile in range(TILES):
                apart = spread(beyond[part], relayed[1 - odd, begin + 7 + part], tile)
                swapped = jnp.where(is_first & near, layer(there, part, tile), apart)
                far1[face, part, tile] = jnp.where(
                    flagged, swapped, relayed[odd, begin + part * TILES + tile]
                )
    choose(lambda face, part, tile: own1[face, part, tile], far1)

    all_x, all_y, all_z = (scale_x, scale_x, scale_c), (scale_y, scale_y, scale_c), (scale_z, scale_z, scale_c)

    def lanes_of(v, index):
        return jnp.take_along_axis(v, index, axis=1)

    def z_layers(half, tile):
        scale, wall = all_x[tile], all_y[tile]
        for side in range(2):
            at = 15 * side
            index = 16 * (lane & 7) + at
            edge = jnp.where(
                (lane & 8) == 0,
                lanes_of(picked[half, 0, tile], index),
                lanes_of(picked[half, 1, tile], index),
            )
            v = faces1[2 + side, half, tile] + all_z[tile] * picked[2 + side, half, tile]
            v = v + jnp.where(high_y if half else low_y, wall * edge, zero)
            v = v + jnp.where(z == 0, scale * roll(chosen[0, half, tile], -at), zero)
            v = v + jnp.where(z == EDGE - 1, scale * roll(chosen[1, half, tile], 15 - at), zero)
            faces1[2 + side, half, tile] = v

    def y_layers(part, tile):
        scale, wall = all_x[tile], all_z[tile]
        for side in range(2):
            index = 112 * side + 8 * part + column
            v = faces1[side, part, tile] + all_y[tile] * picked[side, part, tile]
            v = v + jnp.where(z == 0, wall * lanes_of(picked[2, side, tile], index), zero)
            v = v + jnp.where(z == EDGE - 1, wall * lanes_of(picked[3, side, tile], index), zero)
            plane = roll(chosen[part, side, tile], 112 * part - 112 * side)
            v = v + jnp.where(high_y if part else low_y, scale * plane, zero)
            faces1[side, part, tile] = v

    second = exchange(state1, faces1, ghosts1)
    def advance_at(x):
        for half in range(HALVES):
            for tile in range(TILES):
                v = finish_xy(partial[x, half, tile], x, half, tile)
                state1[x, half, tile] = finish_z(v, x, half, tile)

    for x in order[:2]:
        advance_at(x)
    for part in range(2):
        for tile in range(TILES):
            y_layers(part, tile)
    start(second[:4])
    for part in range(2):
        for tile in range(TILES):
            z_layers(part, tile)
    start(second[4:])
    for x in order[2:]:
        advance_at(x)
    relay_block(is_odd & (odd_grp == 1))
    for x in range(EDGE):
        prepare(state1, x)
    def wait(copies):
        for copy, _, comes in copies:

            @pl.when(comes)
            def _():
                copy.wait_recv()

    def own2(face, part, tile):
        if face < 2:
            return state1[(EDGE - 1) * face, part, tile]
        return faces1[face - 2, part, tile]

    wait(second)
    choose(own2, ghosts1)

    for half in range(HALVES):
        for x in range(EDGE):
            for tile in range(TILES):
                v = finish_xy(partial[x, half, tile], x, half, tile)
                write_rows(out, half, tile, x, finish_z(v, x, half, tile))

    for number, there in (
        (0, is_odd & has_above_grp), (1, is_odd & has_below_grp), (2, is_odd), (3, is_odd)
    ):

        @pl.when(there)
        def _():
            passes[number].wait_send()

    for copy, there, *_ in sends + second:

        @pl.when(there)
        def _():
            copy.wait_send()


def solution(mesh):
    n_grp, n_dev = mesh.shape["grp"], mesh.shape["dev"]

    def body(fields, swap_dev, swap_grp, neighbors, orient):
        block = (HALVES, NFIELD, SLOTS, EDGE, LANES)
        plane = (HALVES, TILES, 8, LANES)
        smalls = (neighbors, orient)
        cells = [(EDGE,) + plane] * 3
        shapes = [block, block, *cells, (PACKED, 8, LANES), (4,) + plane, *[(6,) + plane] * 3, (4,) + plane, *[(2,) + plane] * 3]
        shapes += [(12, 8, LANES), (2, 13, 8, LANES), (2, RELAYED, 8, LANES), (2, HALVES, NFIELD, EDGE, LANES)]
        shapes += [(4, 8, LANES), (4, 8, LANES), (2, 8, LANES)]
        new = pl.pallas_call(
            functools.partial(kernel, n_grp, n_dev),
            out_shape=jax.ShapeDtypeStruct((SLOTS, NFIELD, 2, HALVES, 8, LANES), fields.dtype),
            in_specs=[pl.BlockSpec(memory_space=space) for space in (pl.ANY, pltpu.SMEM, pltpu.SMEM, pl.ANY, pl.ANY)],
            out_specs=pl.BlockSpec(memory_space=pltpu.VMEM),
            scratch_shapes=[pltpu.SMEM(a.shape, a.dtype) for a in smalls]
            + [pltpu.VMEM(shape, jnp.float32) for shape in shapes]
            + [pltpu.SemaphoreType.DMA((n,)) for n in (2, 8, 6, 6, 4, 4, 13, 18)]
            + [pltpu.SemaphoreType.REGULAR],
            compiler_params=pltpu.CompilerParams(
                collective_id=0, has_side_effects=True, vmem_limit_bytes=16 * 2**20
            ),
            name="phase_field_steps",
        )(
            in_hbm(fields), swap_dev, swap_grp, *[in_hbm(a) for a in smalls]
        )
        return new.transpose(0, 1, 2, 4, 3, 5).reshape(fields.shape)

    in_specs = (
        P(("grp", "dev"), None, None, None),
        P(("grp", "dev")),
        P(("grp", "dev")),
        P(("grp", "dev"), None),
        P(("grp", "dev")),
    )
    out_specs = P(("grp", "dev"), None, None, None)
    return jax.shard_map(body, mesh=mesh, in_specs=in_specs, out_specs=out_specs, check_vma=False)
```

```python
import functools
import math

import jax
import jax.numpy as jnp
import numpy as np
from jax import lax
from jax.experimental import pallas as pl
from jax.experimental.pallas import tpu as pltpu
from jax.sharding import PartitionSpec as P

MESH = pl.DeviceIdType.MESH
NORI = 8
EDGE = 16
SLOTS = 4
NFIELD = 6
LANES = 128
HALVES = 2
TILES = 3

phase_rate = 0.05
closure = 0.1
conc_rates = (0.08, 0.04)


def in_hbm(a):
    return pltpu.with_memory_space_constraint(a, pltpu.HBM)


def roll(v, shift):
    shift %= LANES
    return v if shift == 0 else pltpu.roll(v, shift, v.ndim - 1)


def rows_of(ref, half, tile, x):
    start = half * (NFIELD * SLOTS * EDGE) + tile * (8 * EDGE) + x
    flat = ref.reshape(HALVES * NFIELD * SLOTS * EDGE, LANES)
    return flat, pl.ds(start, 8, stride=EDGE)


def read_rows(ref, half, tile, x):
    flat, rows = rows_of(ref, half, tile, x)
    return flat[rows, :]


def read_moved(moved, passed, odd, half, tile, x):
    last = read_rows(moved, half, tile, x)
    blocks = passed.reshape(2 * HALVES * NFIELD * EDGE, LANES)
    start = (odd * HALVES + half) * (NFIELD * EDGE) + 2 * tile * EDGE + x
    row = lax.broadcasted_iota(jnp.int32, (8, LANES), 0)
    upper = jnp.broadcast_to(blocks[pl.ds(start, 1), :], (8, LANES))
    lower = jnp.broadcast_to(blocks[pl.ds(start + EDGE, 1), :], (8, LANES))
    return jnp.where(row == 0, upper, jnp.where(row == 4, lower, last))


def write_rows(ref, half, tile, x, v):
    flat = ref.reshape(HALVES * NFIELD * SLOTS * EDGE, LANES)
    for part in range(2):
        start = (2 * tile + part) * 32 + (x // 8) * 16 + half * 8 + x % 8
        flat[pl.ds(start, 4, stride=NFIELD * 32), :] = v[4 * part : 4 * part + 4]


FACE_AT = (0, 13, 6, 19, 26, 35)
FLAGS_AT = (12, 25, 32, 41)
Z_BLOCK_AT = (33, 42)
FIRST_AT, LAST_AT = 44, 56
SHORT_AT = (0, 4, 2, 6, 8, 10)
PACKED = 68
RELAYED = 30


def kernel(
    n_grp, n_dev, fields, swap_dev, swap_grp, neighbors_hbm, orient_hbm, out,
    neighbors, orient,
    raw, moved, state0, state1, partial, packed, faces1, own1, far1, ghosts1, picked, chosen, walls_y, walls_z,
    short3, beside, relayed, passed, outer3, outer0, beyond,
    small_sem, load_sem, send_sem, recv_sem, pass_send, pass_recv, first_send, first_recv, ready_sem,
):
    grp, dev = lax.axis_index("grp"), lax.axis_index("dev")
    rank = grp * n_dev + dev
    odd, odd_grp = lax.rem(dev, 2), lax.rem(grp, 2)
    even = odd == 0
    even_grp = odd_grp == 0
    pair_dev, pair_grp = dev + 1 - 2 * odd, grp + 1 - 2 * odd_grp
    out_dev, out_grp = dev - 1 + 2 * odd, grp - 1 + 2 * odd_grp
    relay = dev + 1 - odd
    has_below_dev, has_above_dev = dev > 0, dev < n_dev - 1
    has_below_grp, has_above_grp = grp > 0, grp < n_grp - 1
    has_outer = jnp.where(even, has_below_dev, has_above_dev)
    to_last = jnp.where(even, dev + 2, dev - 2)
    from_last = jnp.where(even, dev - 2, dev + 2)
    to_first = jnp.where(even_grp, grp + 2, grp - 2)
    from_first = jnp.where(even_grp, grp - 2, grp + 2)
    has_to_last = (to_last >= 0) & (to_last < n_dev)
    has_from_last = (from_last >= 0) & (from_last < n_dev)
    has_to_first = (to_first >= 0) & (to_first < n_grp)
    has_from_first = (from_first >= 0) & (from_first < n_grp)
    sides = (
        (has_below_dev, {"dev": dev - 1}),
        (has_above_dev, {"dev": dev + 1}),
        (has_below_grp, {"grp": grp - 1}),
        (has_above_grp, {"grp": grp + 1}),
    )
    above_relay = {"grp": grp + 1, "dev": relay}
    below_relay = {"grp": grp - 1, "dev": relay}
    pair_relay = {"grp": pair_grp, "dev": relay}
    outer_pair = {"grp": pair_grp, "dev": out_dev}
    is_odd = odd == 1

    barrier = pltpu.get_barrier_semaphore()
    sources = (
        sides[0], (is_odd & has_above_dev, {"dev": dev + 1}),
        (is_odd & has_below_grp, {"grp": grp - 1, "dev": dev}),
        (is_odd & has_above_grp, {"grp": grp + 1, "dev": dev}),
        (is_odd & has_below_grp, {"grp": grp - 1, "dev": dev - 1}),
        (is_odd & has_above_grp, {"grp": grp + 1, "dev": dev - 1}),
        (has_from_last, {"dev": from_last}),
        (has_outer, outer_pair),
        (has_from_first, {"grp": from_first}),
    )
    for there, target in sources:

        @pl.when(there)
        def _():
            pl.semaphore_signal(barrier, inc=1, device_id=target, device_id_type=MESH)

    smalls = [
        pltpu.make_async_copy(neighbors_hbm, neighbors, small_sem.at[0]),
        pltpu.make_async_copy(orient_hbm, orient, small_sem.at[1]),
    ]
    loads = []
    for half in range(HALVES):
        for slot in range(SLOTS):
            loads.append(
                pltpu.make_async_copy(
                    fields.at[slot, :, :, pl.ds(half * LANES, LANES)],
                    raw.at[half, :, slot],
                    load_sem.at[half * SLOTS + slot],
                )
            )
    for copy in loads + smalls:
        copy.start()

    row = lax.broadcasted_iota(jnp.int32, (8, LANES), 0)
    lane = lax.broadcasted_iota(jnp.int32, (8, LANES), 1)
    slot_of = row & 3
    z = lane & 15
    column = lane >> 4
    low_y, high_y = lane < EDGE, lane >= LANES - EDGE

    def per_slot(scalars):
        last = jnp.full((8, LANES), scalars[SLOTS - 1])
        for slot in range(SLOTS - 1):
            last = jnp.where(slot_of == slot, scalars[slot], last)
        return last

    for copy in smalls:
        copy.wait()
    angle = per_slot([orient[slot] for slot in range(SLOTS)])
    cosine = jnp.zeros((8, LANES), jnp.float32)
    sine = jnp.zeros((8, LANES), jnp.float32)
    for number in range(NORI):
        theta = np.float32(math.pi) * np.float32(number) / np.float32(NORI)
        cosine = jnp.where(angle == number, jnp.float32(np.cos(np.float32(2.0) * theta)), cosine)
        sine = jnp.where(angle == number, jnp.float32(np.sin(np.float32(2.0) * theta)), sine)
    scale_x = phase_rate * (1.0 + 0.5 * cosine)
    scale_y = phase_rate * (1.0 - 0.5 * cosine)
    scale_z = phase_rate * (1.0 + 0.5 * sine)
    scale_c = jnp.where(row < 4, jnp.float32(conc_rates[0]), jnp.float32(conc_rates[1]))
    self_p = 1.0 - 2.0 * (scale_x + scale_y + scale_z)
    self_c = 1.0 - 6.0 * scale_c
    zero = jnp.zeros((8, LANES), jnp.float32)
    scales_x = (scale_x, scale_x, scale_c)
    scales_y = tuple(
        tuple(jnp.where(wall, v, zero) for v in (scale_y, scale_y, scale_c)) for wall in (low_y, high_y)
    )
    scales_z = tuple(jnp.where((z == 0) | (z == EDGE - 1), v, zero) for v in (scale_z, scale_z, scale_c))

    picks = []
    for face in range(6):
        target = per_slot([neighbors[slot, face] for slot in range(SLOTS)])
        source_row = (row & 4) | (target & 3)
        picks.append((target < 0, (target >> 2) == rank, source_row))

    swapped_here = ((slot_of == 0) & (swap_grp[0] == 1)) | (
        (slot_of == SLOTS - 1) & (swap_dev[0] == 1)
    )

    def pack_y(state, put):
        for side in range(2):
            for tile in range(TILES):
                low, high = zero, zero
                for k in range(8):
                    x = side * 8 + k
                    both = jnp.where(lane < 64, state[x, 0, tile], state[x, 1, tile])
                    turned = roll(both, 16 * k)
                    low = jnp.where(column == k, turned, low)
                    high = jnp.where(column == (k + 7) % 8, turned, high)
                put(2, side, tile, low)
                put(3, side, tile, roll(high, 16))

    def pack_z(state, put):
        for half in range(HALVES):
            for tile in range(TILES):
                low, high = zero, zero
                for x in range(EDGE):
                    turned = roll(state[x, half, tile], x)
                    low = jnp.where(z == x, turned, low)
                    high = jnp.where(z == (x + 15) % 16, turned, high)
                put(4, half, tile, low)
                put(5, half, tile, roll(high, -15))

    def exchange(state, faces, ghosts):
        plan = (
            (state.at[EDGE - 1], 0, 1),
            (state.at[0], 1, 0),
            (faces.at[1], 2, 1),
            (faces.at[0], 3, 0),
            (faces.at[3], 4, 3),
            (faces.at[2], 5, 2),
        )
        return [
            (
                pltpu.make_async_remote_copy(
                    src_ref=source,
                    dst_ref=ghosts.at[into],
                    send_sem=send_sem.at[into],
                    recv_sem=recv_sem.at[into],
                    device_id=sides[side][1],
                    device_id_type=MESH,
                ),
                sides[side][0],
                sides[side ^ 1][0],
            )
            for source, into, side in plan
        ]

    def start(copies):
        for copy, there, _ in copies:

            @pl.when(there)
            def _():
                copy.start()

    def choose(own, ghosts, along="xyz"):
        def pick(face, part, tile):
            outer, local, source_row = picks[face]
            near = jnp.take_along_axis(own(face ^ 1, part, tile), source_row, axis=0)
            far = jnp.take_along_axis(ghosts[face, part, tile], source_row, axis=0)
            return jnp.where(outer, own(face, part, tile), jnp.where(local, near, far))

        for part in range(2):
            for tile in range(TILES):
                if along != "z":
                    chosen[0, part, tile] = pick(0, part, tile)
                    chosen[1, part, tile] = pick(1, part, tile)
                    below, above = pick(2, part, tile), pick(3, part, tile)
                    picked[0, part, tile], picked[1, part, tile] = below, above
                    below = roll(below, 16)
                    walls_y[0, part, tile] = jnp.where(column % 2 == 0, above, below)
                    walls_y[1, part, tile] = jnp.where(column % 2 == 1, above, below)
                if along != "xy":
                    below, above = pick(4, part, tile), pick(5, part, tile)
                    picked[2, part, tile], picked[3, part, tile] = below, above
                    below = roll(below, -15)
                    walls_z[0, part, tile] = jnp.where(z % 2 == 0, above, below)
                    walls_z[1, part, tile] = jnp.where(z % 2 == 1, above, below)

    def prepare(state, x):
        v = [[state[x, half, tile] for tile in range(TILES)] for half in range(HALVES)]
        linear = [[None] * TILES for _ in range(HALVES)]
        for tile in range(TILES):
            ups = [roll(v[half][tile], -16) for half in range(HALVES)]
            downs = [roll(v[half][tile], 16) for half in range(HALVES)]
            sums_y = (
                jnp.where(high_y, ups[1], ups[0]) + jnp.where(low_y, zero, downs[0]),
                jnp.where(high_y, zero, ups[1]) + jnp.where(low_y, downs[0], downs[1]),
            )
            for half in range(HALVES):
                sum_z = jnp.where(z == EDGE - 1, zero, roll(v[half][tile], -1)) + jnp.where(
                    z == 0, zero, roll(v[half][tile], 1)
                )
                inner = [state[n, half, tile] for n in (x - 1, x + 1) if 0 <= n < EDGE]
                sum_x = inner[0] + inner[1] if len(inner) == 2 else inner[0]
                if tile < 2:
                    linear[half][tile] = (
                        scale_x * sum_x + scale_y * sums_y[half] + scale_z * sum_z + self_p * v[half][tile]
                    )
                else:
                    linear[half][tile] = scale_c * (sum_x + sums_y[half] + sum_z) + self_c * v[half][tile]
        for half in range(HALVES):
            p, q, c = v[half]
            both = p + q
            total = both + pltpu.roll(both, 4, 0)
            drive = c - pltpu.roll(c, 4, 0)
            shared = (phase_rate * closure) - (phase_rate * closure) * total
            partial[x, half, 0] = (
                linear[half][0]
                + shared
                + (p - p * p) * (2.0 * phase_rate * p - phase_rate + (0.5 * phase_rate) * drive)
            )
            partial[x, half, 1] = (
                linear[half][1]
                + shared
                + (q - q * q) * (2.0 * phase_rate * q - phase_rate + phase_rate * drive)
            )
            partial[x, half, 2] = linear[half][2]

    def finish_xy(v, x, half, tile):
        v = v + scales_y[half][tile] * roll(walls_y[x % 2, x // 8, tile], 16 * (7 - x % 8))
        if x == 0:
            v = v + scales_x[tile] * chosen[0, half, tile]
        if x == EDGE - 1:
            v = v + scales_x[tile] * chosen[1, half, tile]
        return v

    def finish_z(v, x, half, tile):
        return v + scales_z[tile] * roll(walls_z[x % 2, half, tile], 15 - x)

    for copy in loads:
        copy.wait()
    for x in range(EDGE):
        for half in range(HALVES):
            for tile in range(TILES):
                state0[x, half, tile] = read_rows(raw, half, tile, x)

    def put_packed(face, part, tile, v):
        packed[FACE_AT[face] + part * TILES + tile] = v

    def layer(face, part, tile):
        return packed[FACE_AT[face] + part * TILES + tile]

    def shorten(face):
        for part in range(2):
            tiles = [layer(face, part, tile) for tile in range(TILES)]
            first, last = tiles[0], zero
            for tile in range(TILES):
                shift = (tile - (SLOTS - 1)) % 8
                first = jnp.where(slot_of == tile, pltpu.roll(tiles[tile], tile, 0) if tile else tiles[0], first)
                last = jnp.where(slot_of == tile, pltpu.roll(tiles[tile], shift, 0), last)
            packed[FIRST_AT + SHORT_AT[face] + part] = first
            packed[LAST_AT + SHORT_AT[face] + part] = last
            if face >= 4:
                packed[Z_BLOCK_AT[face - 4] + part] = last

    flags = jnp.where(swapped_here, 1.0, zero)
    for at in FLAGS_AT:
        packed[at] = flags
    for part in range(2):
        for tile in range(TILES):
            put_packed(0, part, tile, state0[0, part, tile])
            put_packed(1, part, tile, state0[EDGE - 1, part, tile])
    pack_y(state0, put_packed)
    for face in range(4):
        shorten(face)
    pack_z(state0, put_packed)
    shorten(4)
    shorten(5)

    count = jnp.int32(0)
    for there in (
        has_below_dev & even, has_above_dev, has_below_grp, has_above_grp, has_to_last, has_outer, has_to_first
    ):
        count = count + jnp.where(there, 1, 0)
    pl.semaphore_wait(barrier, count)

    always = rank >= 0

    @pl.when(even)
    def _():
        pl.semaphore_signal(ready_sem, inc=1, device_id={"dev": pair_dev}, device_id_type=MESH)

    sends = []

    def send(source, into, number, slot, there, target):
        copy = pltpu.make_async_remote_copy(
            src_ref=source,
            dst_ref=into,
            send_sem=first_send.at[number],
            recv_sem=first_recv.at[slot],
            device_id=target,
            device_id_type=MESH,
        )

        @pl.when(there)
        def _():
            copy.start()

        sends.append((copy, there))

    def received(into, slot, there):
        @pl.when(there)
        def _():
            pltpu.make_async_remote_copy(
                src_ref=into,
                dst_ref=into,
                send_sem=first_send.at[0],
                recv_sem=first_recv.at[slot],
                device_id={"dev": pair_dev},
                device_id_type=MESH,
            ).wait_recv()


    send(
        packed.at[pl.ds(LAST_AT + jnp.where(even, 4, 0), 4)], outer3, 8, 5, has_to_last, {"dev": to_last}
    )
    send(packed.at[pl.ds(FIRST_AT + jnp.where(even, 0, 4), 4)], outer0, 9, 6, has_outer, outer_pair)
    send(packed.at[pl.ds(26, 9)], relayed.at[odd, pl.ds(12, 9)], 0, 8 + 5 * odd, has_below_grp, below_relay)
    send(packed.at[pl.ds(35, 9)], relayed.at[odd, pl.ds(21, 9)], 1, 9 + 5 * odd, has_above_grp, above_relay)
    send(packed.at[pl.ds(FIRST_AT, 12)], relayed.at[odd, pl.ds(0, 12)], 2, 10 + 5 * odd, always, pair_relay)
    send(packed.at[pl.ds(13 * odd, 13)], beside.at[odd], 3, odd, has_outer, {"dev": out_dev})
    send(
        packed.at[pl.ds(FIRST_AT + jnp.where(even_grp, 10, 8), 2)], beyond, 10, 7, has_to_first, {"grp": to_first}
    )

    for half in range(HALVES):
        lanes = pl.ds(half * LANES, LANES)
        send(
            fields.at[0, :, :, lanes], passed.at[odd, half], 6 + half, 11 + half + 5 * odd, always, pair_relay
        )

    @pl.when(is_odd)
    def _():
        pl.semaphore_wait(ready_sem, 1)

    send(packed.at[pl.ds(13 * (1 - odd), 13)], beside.at[1 - odd], 4, 1 - odd, always, {"dev": pair_dev})
    send(packed.at[pl.ds(LAST_AT, 12)], short3, 5, 2, always, {"dev": pair_dev})
    for half in range(HALVES):
        lanes = pl.ds(half * LANES, LANES)
        send(fields.at[SLOTS - 1, :, :, lanes], moved.at[half, :, SLOTS - 1], 11 + half, 3 + half, always, {"dev": pair_dev})

    passes = [
        pltpu.make_async_remote_copy(
            src_ref=ref,
            dst_ref=ref,
            send_sem=pass_send.at[number],
            recv_sem=pass_recv.at[number],
            device_id={"dev": pair_dev},
            device_id_type=MESH,
        )
        for number, ref in enumerate(
            (
                relayed.at[:, pl.ds(12, 9)],
                relayed.at[:, pl.ds(21, 9)],
                relayed.at[:, pl.ds(0, 12)],
                passed.at[0],
            )
        )
    ]

    def pass_on(number, there):
        @pl.when(there)
        def _():
            passes[number].start()

    def relay_layers(number, there):
        for parity in range(2):
            received(relayed.at[parity, pl.ds(12 + 9 * number, 9)], 8 + number + 5 * parity, there)
        pass_on(number, there)

    def relay_first(there):
        received(relayed.at[0, pl.ds(0, 12)], 10, there)
        pass_on(2, there)

    def relay_block(there):
        for half in range(HALVES):
            received(passed.at[0, half], 11 + half, there)
        pass_on(3, there)

    relay_layers(0, is_odd & has_above_grp)
    received(relayed.at[1, pl.ds(0, 12)], 15, is_odd)
    relay_first(is_odd & even_grp)
    relay_block(is_odd & even_grp)
    for half in range(HALVES):
        received(passed.at[1, half], 16 + half, is_odd)

    @pl.when(even)
    def _():
        passes[3].wait_recv()

    for half in range(HALVES):
        received(moved.at[half, :, SLOTS - 1], 3 + half, always)

    order = (0, EDGE - 1, *range(1, EDGE - 1))
    for x in order:
        for half in range(HALVES):
            for tile in range(TILES):
                state0[x, half, tile] = jnp.where(
                    swapped_here, read_moved(moved, passed, odd, half, tile, x), state0[x, half, tile]
                )
    for x in range(EDGE):
        prepare(state0, x)

    def spread(first, last, tile):
        return jnp.where(
            slot_of == 0, pltpu.roll(first, (8 - tile) % 8, 0) if tile else first, pltpu.roll(last, 3 - tile, 0)
        )

    def put_faces(face, part, tile, v):
        faces1[face - 2, part, tile] = v

    pack_z(partial, put_faces)
    pack_y(partial, put_faces)

    received(short3, 2, always)

    @pl.when(even)
    def _():
        passes[2].wait_recv()

    for face in range(6):
        at = SHORT_AT[face]
        for part in range(2):
            for tile in range(TILES):
                swapped = spread(relayed[odd, at + part], short3[at + part], tile)
                own1[face, part, tile] = jnp.where(swapped_here, swapped, layer(face, part, tile))

    relay_layers(1, is_odd & has_below_grp)
    relay_first(is_odd & (odd_grp == 1))
    for number, there in ((0, even & has_above_grp), (1, even & has_below_grp)):

        @pl.when(there)
        def _():
            passes[number].wait_recv()

    received(beside.at[0], 0, has_above_dev)
    received(beside.at[1], 1, has_below_dev)
    received(outer3, 5, has_from_last)
    received(outer0, 6, has_outer)
    received(beyond, 7, has_from_first)

    is_first = slot_of == 0
    for face in range(4):
        side = face % 2
        there = face ^ 1
        short = SHORT_AT[there] % 4
        near = even if side == 1 else is_odd
        landed = beside.at[1 - side]
        begin = 6 * (face // 2)
        flagged = landed[12] > 0.5
        for part in range(2):
            first = jnp.where(near, relayed[1 - odd, SHORT_AT[there] + part], outer0[short + part])
            for tile in range(TILES):
                mine = layer(there, part, tile)
                apart = spread(first, outer3[short + part], tile)
                swapped = jnp.where(is_first, apart, jnp.where(near, mine, apart))
                far1[face, part, tile] = jnp.where(flagged, swapped, landed[begin + part * TILES + tile])
    for face in (4, 5):
        there = face ^ 1
        begin = 12 if face == 5 else 21
        near = even_grp if face == 5 else odd_grp == 1
        flagged = relayed[odd, begin + 6] > 0.5
        for part in range(2):
            for tile in range(TILES):
                apart = spread(beyond[part], relayed[1 - odd, begin + 7 + part], tile)
                swapped = jnp.where(is_first & near, layer(there, part, tile), apart)
                far1[face, part, tile] = jnp.where(
                    flagged, swapped, relayed[odd, begin + part * TILES + tile]
                )
    choose(lambda face, part, tile: own1[face, part, tile], far1)

    all_x, all_y, all_z = (scale_x, scale_x, scale_c), (scale_y, scale_y, scale_c), (scale_z, scale_z, scale_c)

    def lanes_of(v, index):
        return jnp.take_along_axis(v, index, axis=1)

    def z_layers(half, tile):
        scale, wall = all_x[tile], all_y[tile]
        for side in range(2):
            at = 15 * side
            index = 16 * (lane & 7) + at
            edge = jnp.where(
                (lane & 8) == 0,
                lanes_of(picked[half, 0, tile], index),
                lanes_of(picked[half, 1, tile], index),
            )
            v = faces1[2 + side, half, tile] + all_z[tile] * picked[2 + side, half, tile]
            v = v + jnp.where(high_y if half else low_y, wall * edge, zero)
            v = v + jnp.where(z == 0, scale * roll(chosen[0, half, tile], -at), zero)
            v = v + jnp.where(z == EDGE - 1, scale * roll(chosen[1, half, tile], 15 - at), zero)
            faces1[2 + side, half, tile] = v

    def y_layers(part, tile):
        scale, wall = all_x[tile], all_z[tile]
        for side in range(2):
            index = 112 * side + 8 * part + column
            v = faces1[side, part, tile] + all_y[tile] * picked[side, part, tile]
            v = v + jnp.where(z == 0, wall * lanes_of(picked[2, side, tile], index), zero)
            v = v + jnp.where(z == EDGE - 1, wall * lanes_of(picked[3, side, tile], index), zero)
            plane = roll(chosen[part, side, tile], 112 * part - 112 * side)
            v = v + jnp.where(high_y if part else low_y, scale * plane, zero)
            faces1[side, part, tile] = v

    second = exchange(state1, faces1, ghosts1)
    def advance_at(x):
        for half in range(HALVES):
            for tile in range(TILES):
                v = finish_xy(partial[x, half, tile], x, half, tile)
                state1[x, half, tile] = finish_z(v, x, half, tile)

    for x in order[:2]:
        advance_at(x)
    for part in range(2):
        for tile in range(TILES):
            y_layers(part, tile)
    start(second[:4])
    for part in range(2):
        for tile in range(TILES):
            z_layers(part, tile)
    start(second[4:])
    for x in order[2:]:
        advance_at(x)
    relay_block(is_odd & (odd_grp == 1))
    for x in range(EDGE):
        prepare(state1, x)
    def wait(copies):
        for copy, _, comes in copies:

            @pl.when(comes)
            def _():
                copy.wait_recv()

    def own2(face, part, tile):
        if face < 2:
            return state1[(EDGE - 1) * face, part, tile]
        return faces1[face - 2, part, tile]

    for number, there in (
        (0, is_odd & has_above_grp), (1, is_odd & has_below_grp), (2, is_odd), (3, is_odd)
    ):

        @pl.when(there)
        def _():
            passes[number].wait_send()

    for copy, there in sends:

        @pl.when(there)
        def _():
            copy.wait_send()

    wait(second)
    choose(own2, ghosts1)

    for half in range(HALVES):
        for x in range(EDGE):
            for tile in range(TILES):
                v = finish_xy(partial[x, half, tile], x, half, tile)
                write_rows(out, half, tile, x, finish_z(v, x, half, tile))

    for copy, there, _ in second:

        @pl.when(there)
        def _():
            copy.wait_send()


def solution(mesh):
    n_grp, n_dev = mesh.shape["grp"], mesh.shape["dev"]

    def body(fields, swap_dev, swap_grp, neighbors, orient):
        block = (HALVES, NFIELD, SLOTS, EDGE, LANES)
        plane = (HALVES, TILES, 8, LANES)
        smalls = (neighbors, orient)
        cells = [(EDGE,) + plane] * 3
        shapes = [block, block, *cells, (PACKED, 8, LANES), (4,) + plane, *[(6,) + plane] * 3, (4,) + plane, *[(2,) + plane] * 3]
        shapes += [(12, 8, LANES), (2, 13, 8, LANES), (2, RELAYED, 8, LANES), (2, HALVES, NFIELD, EDGE, LANES)]
        shapes += [(4, 8, LANES), (4, 8, LANES), (2, 8, LANES)]
        new = pl.pallas_call(
            functools.partial(kernel, n_grp, n_dev),
            out_shape=jax.ShapeDtypeStruct((SLOTS, NFIELD, 2, HALVES, 8, LANES), fields.dtype),
            in_specs=[pl.BlockSpec(memory_space=space) for space in (pl.ANY, pltpu.SMEM, pltpu.SMEM, pl.ANY, pl.ANY)],
            out_specs=pl.BlockSpec(memory_space=pltpu.VMEM),
            scratch_shapes=[pltpu.SMEM(a.shape, a.dtype) for a in smalls]
            + [pltpu.VMEM(shape, jnp.float32) for shape in shapes]
            + [pltpu.SemaphoreType.DMA((n,)) for n in (2, 8, 6, 6, 4, 4, 13, 18)]
            + [pltpu.SemaphoreType.REGULAR],
            compiler_params=pltpu.CompilerParams(
                collective_id=0, has_side_effects=True, vmem_limit_bytes=16 * 2**20
            ),
            name="phase_field_steps",
        )(
            in_hbm(fields), swap_dev, swap_grp, *[in_hbm(a) for a in smalls]
        )
        return new.transpose(0, 1, 2, 4, 3, 5).reshape(fields.shape)

    in_specs = (
        P(("grp", "dev"), None, None, None),
        P(("grp", "dev")),
        P(("grp", "dev")),
        P(("grp", "dev"), None),
        P(("grp", "dev")),
    )
    out_specs = P(("grp", "dev"), None, None, None)
    return jax.shard_map(body, mesh=mesh, in_specs=in_specs, out_specs=out_specs, check_vma=False)
```
